256 devices in a mesh: gx: 16 (over z, x_hi), gy: 16 (over x_lo, y, core).
Axes of the slice: x: 4 (x_hi: 2, x_lo: 2; x = x_hi * 2 + x_lo), y: 4, z: 8, core: 2. Of those that a mesh axis runs over, the one named last changes fastest.
Arguments:
- features: bfloat16 [32, 32, 16, 128], P('gx', 'gy'), may hold values from -6 to 6
- positions: float32 [32, 32, 3, 16], P('gx', 'gy')
- species: int32 [32, 32, 16], P('gx', 'gy'), may hold values from 0 to 5
- neighbours: int32 [32, 32, 16, 32], P('gx', 'gy'), may hold values from 0 to 143, as said below
- counts: int32 [32, 32, 16], P('gx', 'gy'), may hold values from 0 to 32, as said below
- species_gain: float32 [6, 128], replicated, may hold values from 0.1 to 1.9
- radial_in: float32 [2, 8, 64], replicated, may hold values from -4 to 4
- radial_out: float32 [2, 64, 384], replicated, may hold values from -1 to 1
- mixing: float32 [2, 384, 128], replicated, may hold values from -0.3125 to 0.3125
- readout: float32 [128], replicated, may hold values from -0.5 to 0.5
Outputs:
- energy: float32 [32, 32, 16], P('gx', 'gy')
- forces: float32 [32, 32, 3, 16], P('gx', 'gy')
- feature_grad: float32 [32, 32, 16, 128], P('gx', 'gy')
The draws below stay inside these ranges and needn't reach their ends.
Inputs may be any that keep to these rules, and one draw needn't show every extreme that they name: `neighbours`: A code n names the atom in slot n % 16 of the column displaced by ((n // 16) // 3 - 1, (n // 16) % 3 - 1) columns, periodically; the codes of one atom are distinct and never name the atom itself. Neighbour slots 0 to counts - 1 of an atom are live, the rest padding.
All inputs are finite; a program needn't handle non-finite values.
Results may differ from the reference program's by a relative error of at most 0.007.
Values may be sent and summed in bfloat16 or wider, within the bound.
A program may use at most 64 MiB of HBM per device.

```python
import jax
import jax.numpy as jnp
from jax import lax

SLOTS = 16
NEIGH = 32
CHANNELS = 128
RADIAL = 64
BASIS = 8
KINDS = 6
LAYERS = 2
GRID_X = 32
GRID_Y = 32


def lattice_sites(key):
    column_count = GRID_X * GRID_Y
    column_keys = jax.random.split(jax.random.fold_in(key, 31), column_count)
    orders = jax.vmap(lambda single: jax.random.permutation(single, 64))(column_keys)
    chosen = orders[:, :SLOTS].astype(jnp.int32).reshape(GRID_X, GRID_Y, SLOTS)
    return (chosen // 16, chosen // 4 % 4, chosen % 4)


def neighbour_table(key):
    site_x, site_y, site_z = lattice_sites(key)
    cand_x = []
    cand_y = []
    cand_z = []
    for offset in range(9):
        step_x = offset // 3 - 1
        step_y = offset % 3 - 1
        cand_x.append(jnp.roll(site_x, (-step_x, -step_y), (0, 1)) + 4 * step_x)
        cand_y.append(jnp.roll(site_y, (-step_x, -step_y), (0, 1)) + 4 * step_y)
        cand_z.append(jnp.roll(site_z, (-step_x, -step_y), (0, 1)))
    far_x = jnp.stack(cand_x, axis=2).reshape(GRID_X, GRID_Y, 1, 9 * SLOTS)
    far_y = jnp.stack(cand_y, axis=2).reshape(GRID_X, GRID_Y, 1, 9 * SLOTS)
    far_z = jnp.stack(cand_z, axis=2).reshape(GRID_X, GRID_Y, 1, 9 * SLOTS)
    diff_x = far_x - site_x[..., None]
    diff_y = far_y - site_y[..., None]
    diff_z = far_z - site_z[..., None]
    lattice_sq = diff_x * diff_x + diff_y * diff_y + diff_z * diff_z
    codes = jnp.arange(9 * SLOTS, dtype=jnp.int32)
    self_code = 4 * SLOTS + jnp.arange(SLOTS, dtype=jnp.int32)
    is_self = codes[None, None, None, :] == self_code[None, None, :, None]
    within = jnp.logical_and(lattice_sq <= 5, jnp.logical_not(is_self))
    scores = jnp.where(within, lattice_sq * 1024 + codes, lattice_sq * 1024 + 1073741824 + codes)
    scores = jnp.where(is_self, 2 * 1073741824 - 1, scores)
    ranked = jnp.argsort(scores, axis=-1)[..., :NEIGH].astype(jnp.int32)
    live = jnp.minimum(jnp.sum(within.astype(jnp.int32), axis=-1), NEIGH).astype(jnp.int32)
    live = live.at[0, 0, 0].set(NEIGH)
    return (ranked, live)


def draw_neighbours(key, part):
    ranked, live = neighbour_table(key)
    return ranked


def draw_counts(key, part):
    ranked, live = neighbour_table(key)
    return live


def draw_positions(key, part):
    site_x, site_y, site_z = lattice_sites(key)
    centres = jnp.stack([site_x, site_y, site_z], axis=2).astype(jnp.float32)
    centres = (centres + 0.5) * 1.5
    jitter_key = jax.random.fold_in(key, 47)
    jitter = jnp.clip(0.1 * jax.random.normal(jitter_key, centres.shape, jnp.float32), -0.3, 0.3)
    return (centres + jitter).astype(jnp.float32)


def touch_ends(array, stream_key, least, largest):
    longest = array.shape.index(max(array.shape))
    spots = []
    for shift in (0, 1):
        where = [jax.random.randint(jax.random.fold_in(stream_key, axis), (), 0, length) for axis, length in enumerate(array.shape)]
        where[longest] = (where[longest] + shift) % array.shape[longest]
        spots.append(tuple(where))
    return array.at[spots[0]].set(least).at[spots[1]].set(largest)


def level_of(stream_key, shape, cuts, least, largest):
    gain, own = 1.0, jax.random.fold_in(stream_key, 6)
    for position, blocks in cuts:
        draws = jnp.exp(jax.random.uniform(jax.random.fold_in(own, position), (blocks,), jnp.float32, least / len(cuts), largest / len(cuts)))
        gain = gain * jnp.repeat(draws, shape[position] // blocks).reshape([-1 if axis == position else 1 for axis in range(len(shape))])
    return gain


def normal_values(rng, shape, deviation, reach, pieces=(), kind=jnp.bfloat16):
    result = deviation * jax.random.normal(rng, shape, jnp.float32)
    if pieces:
        result = result * level_of(rng, shape, pieces, -0.22, 0.18)
    return jnp.clip(result, -reach, reach).astype(kind)


def setup_inputs(seed: int = 0) -> dict:
    streams_of = jax.random.split(jax.random.key(seed), 11)
    return {
        "features": normal_values(streams_of[0], (GRID_X, GRID_Y, SLOTS, CHANNELS), 1.0, 6.0, ((0, 16), (1, 16))),
        "positions": draw_positions(jax.random.fold_in(streams_of[10], 71), 0),
        "species": touch_ends(jax.random.randint(streams_of[2], (GRID_X, GRID_Y, SLOTS), 0, KINDS), jax.random.fold_in(streams_of[2], 1), 0, KINDS - 1).astype(jnp.int32),
        "neighbours": draw_neighbours(jax.random.fold_in(streams_of[10], 71), 0),
        "counts": draw_counts(jax.random.fold_in(streams_of[10], 71), 0),
        "species_gain": jnp.clip(1.0 + 0.18 * jax.random.normal(streams_of[5], (KINDS, CHANNELS), jnp.float32), 0.1, 1.9),
        "radial_in": normal_values(streams_of[6], (LAYERS, BASIS, RADIAL), (BASIS // 4) ** -0.5, 4.0, (), jnp.float32),
        "radial_out": normal_values(streams_of[7], (LAYERS, RADIAL, 3 * CHANNELS), (RADIAL // 2) ** -0.5, 1.0, (), jnp.float32),
        "mixing": normal_values(streams_of[8], (LAYERS, 3 * CHANNELS, CHANNELS), (3 * CHANNELS) ** -0.5, 0.3125, (), jnp.float32),
        "readout": normal_values(streams_of[9], (CHANNELS,), CHANNELS ** -0.5, 0.5, (), jnp.float32),
    }


column = 6.0
cutoff = 6.0
softening = 0.01
root_three = 3.0 ** 0.5
highest = lax.Precision.HIGHEST

def harmonics(unit_x, unit_y, unit_z):
    square = unit_x * unit_x + unit_y * unit_y + unit_z * unit_z
    return jnp.stack([jnp.ones_like(unit_x), unit_x, unit_y, unit_z, root_three * unit_x * unit_y, root_three * unit_y * unit_z, 0.5 * (3.0 * unit_z * unit_z - square), root_three * unit_x * unit_z, 0.5 * root_three * (unit_x * unit_x - unit_y * unit_y)], axis=1)

def layer_block(own_x, own_y, own_z, own_feat, other_x, other_y, other_z, other_feat, live_mask, weights):
    weight_in, weight_out, weight_mix = weights
    sep_x = other_x - own_x[:, None]
    sep_y = other_y - own_y[:, None]
    sep_z = other_z - own_z[:, None]
    dist_sq = sep_x * sep_x + sep_y * sep_y + sep_z * sep_z
    distance = jnp.sqrt(dist_sq + softening)
    envelope = jnp.square(jnp.maximum(1.0 - dist_sq / (cutoff * cutoff), 0.0)) * live_mask
    basis_count = weight_in.shape[0]
    spacing = cutoff / (basis_count - 1)
    centres = spacing * jnp.arange(basis_count, dtype=jnp.float32)
    radial_basis = jnp.exp(-jnp.square((distance[..., None] - centres) / spacing))
    hidden = jax.nn.silu(jnp.einsum('bkn,nh->bkh', radial_basis, weight_in, precision=highest))
    radial = jnp.einsum('bkh,hq->bkq', hidden, weight_out, precision=highest) * envelope[..., None]
    channels = other_feat.shape[-1]
    angular = harmonics(sep_x / cutoff, sep_y / cutoff, sep_z / cutoff)
    scalar = jnp.einsum('bmk,bkc->bmc', angular[:, 0:1], radial[..., :channels] * other_feat, precision=highest)[:, 0]
    vector = jnp.einsum('bmk,bkc->bmc', angular[:, 1:4], radial[..., channels:2 * channels] * other_feat, precision=highest)
    tensor = jnp.einsum('bmk,bkc->bmc', angular[:, 4:9], radial[..., 2 * channels:] * other_feat, precision=highest)
    invariants = jnp.concatenate([scalar, lax.optimization_barrier(jnp.sum(vector * vector, axis=1)), lax.optimization_barrier(jnp.sum(tensor * tensor, axis=1))], axis=-1)
    return jnp.dot(invariants, weight_mix, precision=highest) + own_feat

def layer(pos_all, feat_all, own_pos, own_feat, edge_lists, weights):
    channels = feat_all.shape[-1]
    slot_count = own_feat.shape[2]
    columns = own_feat.shape[0] * own_feat.shape[1]
    flat_x = pos_all[:, :, 0, :].reshape(-1)
    flat_y = pos_all[:, :, 1, :].reshape(-1)
    flat_z = pos_all[:, :, 2, :].reshape(-1)
    flat_feat = feat_all.reshape(-1, channels)
    owned = (own_pos[:, :, 0, :].reshape(columns, slot_count), own_pos[:, :, 1, :].reshape(columns, slot_count), own_pos[:, :, 2, :].reshape(columns, slot_count), own_feat.reshape(columns, slot_count, channels))

    def one_column(column_items):
        other_index, move_x, move_y, live_mask, own_x, own_y, own_z, own_rows = column_items
        return layer_block(own_x, own_y, own_z, own_rows, flat_x[other_index] + move_x, flat_y[other_index] + move_y, flat_z[other_index], flat_feat[other_index], live_mask, weights)
    return lax.map(jax.checkpoint(one_column), edge_lists + owned).reshape(-1, channels)

def reference(features, positions, species, neighbours, counts, species_gain, radial_in, radial_out, mixing, readout):
    kind_count = species_gain.shape[0]
    onehot = (species[..., None] == jnp.arange(kind_count, dtype=jnp.int32)).astype(jnp.float32)
    gain_rows = jnp.einsum('abse,ec->absc', onehot, species_gain, precision=highest)
    layer_one = (features.astype(jnp.float32) * gain_rows).astype(jnp.bfloat16)
    offsets = neighbours // SLOTS
    slot_of = neighbours % SLOTS
    step_x = offsets // 3 - 1
    step_y = offsets % 3 - 1
    col_x = jnp.arange(GRID_X, dtype=jnp.int32)[:, None, None, None]
    col_y = jnp.arange(GRID_Y, dtype=jnp.int32)[None, :, None, None]
    other_atom = ((col_x + step_x) % GRID_X * GRID_Y + (col_y + step_y) % GRID_Y) * SLOTS + slot_of
    shift_x = step_x.astype(jnp.float32) * column
    shift_y = step_y.astype(jnp.float32) * column
    validity = (jnp.arange(NEIGH, dtype=jnp.int32) < counts[..., None]).astype(jnp.float32)
    columns = GRID_X * GRID_Y
    edge_lists = (other_atom.reshape(columns, SLOTS, NEIGH), shift_x.reshape(columns, SLOTS, NEIGH), shift_y.reshape(columns, SLOTS, NEIGH), validity.reshape(columns, SLOTS, NEIGH))
    weights_one = (radial_in[0], radial_out[0], mixing[0])
    weights_two = (radial_in[1], radial_out[1], mixing[1])

    def first_layer(coords, values):
        return layer(coords, values, coords, values, edge_lists, weights_one)

    def second_layer(coords, values):
        return layer(coords, values, coords, values, edge_lists, weights_two)
    z_one, back_one = jax.vjp(first_layer, positions, layer_one.astype(jnp.float32))
    layer_two = z_one.astype(jnp.bfloat16).reshape(GRID_X, GRID_Y, SLOTS, CHANNELS)
    z_two, back_two = jax.vjp(second_layer, positions, layer_two.astype(jnp.float32))
    energy = jnp.dot(jax.nn.silu(z_two), readout, precision=highest)
    sigmoid = jax.nn.sigmoid(z_two)
    z_grad = sigmoid * (1.0 + z_two * (1.0 - sigmoid)) * readout
    pos_two, feat_two = back_two(z_grad)
    pos_one, feat_one = back_one(feat_two.reshape(-1, CHANNELS))
    forces = -(pos_one + pos_two)
    return (energy.reshape(GRID_X, GRID_Y, SLOTS), forces, feat_one)
```

```python
import functools

import jax
import jax.numpy as jnp
from jax import lax
from jax.experimental import pallas as pl
from jax.experimental.pallas import tpu as pltpu
from jax.sharding import PartitionSpec as P

F32 = jnp.float32
BF16 = jnp.bfloat16
MESH = pl.DeviceIdType.MESH
GRAD = BF16
DIRS = tuple((dx, dy) for dx in (-1, 0, 1) for dy in (-1, 0, 1) if (dx, dy) != (0, 0))
SPACING = 6.0 / 7.0
ROOT3 = 3.0**0.5
GROUPS = 8
PARTS = ((0, 8, 1, 0), (16, 24, 3, 1), (64, 40, 5, 4))


def nn(a, b):
    return lax.dot_general(a, b, (((1,), (0,)), ((), ())), preferred_element_type=F32)


def nt(a, b):
    return lax.dot_general(a, b, (((1,), (1,)), ((), ())), preferred_element_type=F32)


def tn(a, b):
    return lax.dot_general(a, b, (((0,), (0,)), ((), ())), preferred_element_type=F32)


def hi_lo(x):
    hi = x.astype(BF16).astype(F32)
    return hi, x - hi


def three(x):
    hi, rest = hi_lo(x)
    mid, low = hi_lo(rest)
    return hi, mid, low


def iota(shape, dim):
    return lax.broadcasted_iota(jnp.int32, shape, dim)


def kernel(
    nx, ny,
    feat, pos, spec, nb, cnt, gain, w_in, w_out, mix, readout,
    energy, forces, fgrad,
    tab1, tab2, postab, gs2, gr2, gs1, gr1, ps, pr,
    oh, amat, geo, atom, idx_ref, hid, dse, rad, pbf, xjt, msg, inv, dinv, acc, grad,
    wo3, w3, woc, mixc, tabt,
    ssem, rsem,
):
    gx, gy = lax.axis_index("gx"), lax.axis_index("gy")
    peers = [(lax.rem(gx + (dx + nx), nx), lax.rem(gy + (dy + ny), ny)) for dx, dy in DIRS]

    barrier = pltpu.get_barrier_semaphore()
    for peer in peers:
        pl.semaphore_signal(barrier, inc=1, device_id=peer, device_id_type=MESH)

    def pick(d, up, down, mid):
        return up if d == 1 else down if d == -1 else mid

    def copies(slot, src, dst, src_at, dst_at):
        out = []
        for k, (dx, dy) in enumerate(DIRS):
            out.append(
                pltpu.make_async_remote_copy(
                    src_ref=src.at[src_at(dx), src_at(dy)],
                    dst_ref=dst.at[dst_at(dx), dst_at(dy)],
                    send_sem=ssem.at[slot, k],
                    recv_sem=rsem.at[slot, k],
                    device_id=peers[k],
                    device_id_type=MESH,
                )
            )
        return out

    centre = pl.ds(1, 2)

    def owned_at(d):
        return pick(d, 2, 1, centre)

    def halo_at(d):
        return pick(d, 0, 3, centre)

    def ghost_at(d):
        return pick(d, 3, 0, centre)

    def input_at(d):
        return pick(d, 1, 0, pl.ds(0, 2))

    send_pos = copies(0, pos, postab, input_at, halo_at)
    send_one = copies(1, tab1, tab1, owned_at, halo_at)
    send_two = copies(2, tab2, tab2, owned_at, halo_at)
    back_two = copies(3, gs2, gr2, ghost_at, halo_at)
    back_one = copies(4, gs1, gr1, ghost_at, halo_at)
    back_pos = copies(5, ps, pr, ghost_at, halo_at)

    def start(group):
        for copy in group:
            copy.start()

    def arrive(group):
        for copy in group:
            copy.wait_recv()

    kinds = gain.shape[0]
    for cx in range(2):
        for cy in range(2):
            onehot = (iota((kinds, 16), 0) == spec[cx, cy : cy + 1, :]).astype(F32)
            rows = lax.dot_general(
                onehot, gain[...], (((0,), (0,)), ((), ())),
                precision=lax.Precision.HIGHEST, preferred_element_type=F32,
            )
            tab1[1 + cx, 1 + cy] = (feat[cx, cy].astype(F32) * rows).astype(BF16)

    for g in range(GROUPS):
        cx, cy = g // 4, g // 2 % 2
        atom[0, g : g + 1, :] = cnt[cx, cy : cy + 1, :].astype(F32)
        for comp in range(3):
            atom[1 + comp, g : g + 1, :] = pos[cx, cy, comp : comp + 1, :]

    sub = iota((8, 256), 0)
    lane = iota((8, 256), 1)
    lane_atom = lax.shift_right_logical(lane, 5)
    diag = (sub == lane_atom).astype(F32)
    half16 = (lax.shift_right_logical(iota((8, 16), 1), 3) == (iota((8, 16), 0) & 1)).astype(F32)
    spread = (
        (iota((16, 256), 0) & 7) == lax.shift_right_logical(iota((16, 256), 1), 5)
    ).astype(BF16)
    pieces = [atom[0] * half16, jnp.zeros((8, 16), F32)]
    for comp in range(3):
        pieces += list(three(atom[1 + comp] * half16))
    pieces += [jnp.zeros((8, 16), F32)]
    wide = nn(jnp.concatenate(pieces, axis=0).astype(BF16), spread)
    count = wide[0:8]
    own = []
    for comp in range(3):
        at = 16 + 24 * comp
        own.append(wide[at : at + 8] + (wide[at + 8 : at + 16] + wide[at + 16 : at + 24]))
    live = ((lane & 31).astype(F32) < count).astype(F32)

    codes = nb[...].reshape(64, 32).astype(F32).astype(BF16)
    tile = (iota((32, 256), 0) == (iota((32, 256), 1) & 31)).astype(BF16)
    repeated = nn(codes, tile)
    keep = (iota((64, 256), 0) & 7) == lax.shift_right_logical(iota((64, 256), 1), 5)
    repeated = jnp.where(keep, repeated, 0.0).astype(BF16)
    gather8 = (iota((8, 64), 0) == lax.shift_right_logical(iota((8, 64), 1), 3)).astype(BF16)
    code = nn(gather8, repeated).astype(jnp.int32)
    offset = lax.shift_right_logical(code, 4)
    step_x = (offset >= 3).astype(jnp.int32) + (offset >= 6).astype(jnp.int32)
    step_y = offset - 3 * step_x
    halo_x = lax.shift_right_logical(sub, 2) + step_x
    halo_y = (lax.shift_right_logical(sub, 1) & 1) + step_y
    idx_ref[...] = (halo_x * 4 + halo_y) * 16 + (code & 15)

    pl.semaphore_wait(barrier, len(DIRS))
    start(send_pos)
    start(send_one)

    def groups(body):
        def pair(t, carry):
            body(2 * t)
            body(2 * t + 1)
            return carry

        lax.fori_loop(0, GROUPS // 2, pair, 0)

    def make_onehot(g):
        row = idx_ref[pl.ds(g, 1), :]
        oh[g] = (iota((256, 256), 0) == row).astype(F32).astype(BF16)

    groups(make_onehot)

    for t in range(2):
        hi, low = hi_lo(w_out[t])
        woc[t] = jnp.concatenate([hi, low], axis=0).astype(BF16)
        wo3[t] = jnp.concatenate([hi, hi, low, low], axis=0).T.astype(BF16)
        hi, low = hi_lo(w_in[t])
        w3[t] = jnp.concatenate([hi, hi, low, low], axis=0).astype(BF16)
        hi, low = hi_lo(mix[t])
        mixc[t] = jnp.concatenate([hi, low], axis=1).astype(BF16)
    for cx in range(2):
        for cy in range(2):
            postab[1 + cx, 1 + cy] = pos[cx, cy]

    arrive(send_pos)
    spots = [postab[hx, hy] for hx in range(4) for hy in range(4)]
    lanes = jnp.concatenate(spots, axis=1)
    lanes = jnp.concatenate([lanes, jnp.zeros((5, 256), F32)], axis=0)
    split = jnp.concatenate(list(three(lanes)) + [jnp.zeros((8, 256), F32)], axis=0).astype(BF16)
    for g in range(GROUPS):
        found = nn(split, oh[g])
        found = found[0:8] + (found[8:16] + found[16:24])
        for comp in range(3):
            geo[comp, g : g + 1, :] = found[comp : comp + 1]
    sep_x = geo[0] + 6.0 * (step_x - 1).astype(F32) - own[0]
    sep_y = geo[1] + 6.0 * (step_y - 1).astype(F32) - own[1]
    sep_z = geo[2] - own[2]
    dist_sq = sep_x * sep_x + sep_y * sep_y + sep_z * sep_z
    distance = jnp.sqrt(dist_sq + 0.01)
    inside = jnp.maximum(1.0 - dist_sq / 36.0, 0.0)
    ux, uy, uz = sep_x / 6.0, sep_y / 6.0, sep_z / 6.0
    angular = [
        jnp.ones_like(ux), ux, uy, uz,
        ROOT3 * ux * uy, ROOT3 * uy * uz, uz * uz - 0.5 * (ux * ux + uy * uy), ROOT3 * ux * uz,
        0.5 * ROOT3 * (ux * ux - uy * uy),
    ]
    geo[0] = distance / SPACING
    geo[1] = inside * inside * live
    for m in range(9):
        geo[2 + m] = angular[m]

    def make_harmonics(g):
        rows = []
        for _, _, parts, first in PARTS:
            split_rows = [hi_lo(geo[2 + first + m, pl.ds(g, 1), :] * diag) for m in range(parts)]
            rows += [hi for hi, _ in split_rows] + [low for _, low in split_rows]
        amat[g] = jnp.concatenate(rows, axis=0).astype(BF16)

    groups(make_harmonics)

    order = iota((8, 256), 0).astype(F32)

    def radial(t, g):
        arg = geo[0, pl.ds(g, 1), :] - order
        envelope = geo[1, pl.ds(g, 1), :]
        hi, low = hi_lo(jnp.exp(-(arg * arg)))
        pre = tn(w3[t], jnp.concatenate([hi, low, hi, low], axis=0).astype(BF16))
        sig = 0.5 * jnp.tanh(0.5 * pre) + 0.5
        silu = pre * sig
        hid[t, g] = silu
        dse[t, g] = (sig + silu * (1.0 - sig)) * envelope
        hi, low = hi_lo(silu * envelope)
        rad[t, g] = nn(wo3[t], jnp.concatenate([hi, low, hi, low], axis=0).astype(BF16))

    def gather_table(table):
        tabt[...] = table[...].reshape(256, 128).astype(F32).T.astype(BF16)

    def messages(t, g):
        found = nn(tabt[...], oh[g])
        xjt[t, g] = found
        for part, (at, rows, parts, first) in enumerate(PARTS):
            prod = (rad[t, g, 128 * part : 128 * part + 128, :] * found).astype(BF16)
            pbf[t, g, 128 * part : 128 * part + 128, :] = prod
            both = nt(amat[g, at : at + 2 * rows, :], prod)
            got = both[:rows] + both[rows:]
            msg[t, g, 8 * first : 8 * first + rows, :] = got
            if part == 0:
                total = got
            else:
                square = got * got
                total = square[0:8]
                for m in range(1, parts):
                    total = total + square[8 * m : 8 * m + 8]
            inv[pl.ds(pl.multiple_of(8 * g, 8), 8), 128 * part : 128 * part + 128] = total

    def mixed(t):
        hi, low = hi_lo(inv[...])
        both = nn(jnp.concatenate([hi, low], axis=0).astype(BF16), mixc[t])
        return (both[64:, :128] + both[:64, 128:]) + both[:64, :128]

    def unmixed(t, cotangent):
        hi, low = hi_lo(cotangent)
        left = jnp.concatenate(
            [jnp.concatenate([hi, hi], axis=1), jnp.concatenate([low, low], axis=1)], axis=0
        ).astype(BF16)
        both = nt(left, mixc[t])
        dinv[...] = both[:64] + both[64:]

    def message_grads(t, g, part):
        at, rows, parts, first = PARTS[part]
        base = dinv[pl.ds(pl.multiple_of(8 * g, 8), 8), 128 * part : 128 * part + 128]
        if part == 0:
            return base
        base = base + base
        return jnp.concatenate(
            [msg[t, g, 8 * (first + m) : 8 * (first + m) + 8, :] * base for m in range(parts)],
            axis=0,
        )

    def product_grad(t, g, part, got):
        at, rows, parts, first = PARTS[part]
        return tn(
            jnp.concatenate([got, got], axis=0).astype(BF16), amat[g, at : at + 2 * rows, :]
        )

    def scatter(t, g):
        total = None
        for part in range(3):
            dp = product_grad(t, g, part, message_grads(t, g, part))
            term = dp * rad[t, g, 128 * part : 128 * part + 128, :]
            total = term if total is None else total + term
        hi, low = hi_lo(total)
        acc[...] += nt(oh[g], jnp.concatenate([hi, low], axis=0).astype(BF16))

    def scattered():
        return acc[:, :128] + acc[:, 128:]

    def coordinate_grads(t, g):
        found = xjt[t, g]
        spread_rows = []
        dr = []
        for part, (at, rows, parts, first) in enumerate(PARTS):
            got = message_grads(t, g, part)
            dr.append((product_grad(t, g, part, got) * found).astype(BF16))
            hi, low = hi_lo(got)
            cross = nn(
                jnp.concatenate([hi, low], axis=0).astype(BF16),
                pbf[t, g, 128 * part : 128 * part + 128, :],
            )
            cross = cross[:rows] + cross[rows:]
            for m in range(parts):
                spread_rows.append(
                    jnp.sum(cross[8 * m : 8 * m + 8] * diag, axis=0, keepdims=True)
                )
        both = nn(woc[t], jnp.concatenate(dr, axis=0))
        dhid = both[:64] + both[64:]
        denv = jnp.sum(dhid * hid[t, g], axis=0, keepdims=True)
        hi, low = hi_lo(dhid * dse[t, g])
        dpre = jnp.concatenate([hi, low, hi, low], axis=0).astype(BF16)
        wide_in = w3wide[t]
        dbasis = nn(wide_in, dpre)
        arg = geo[0, pl.ds(g, 1), :] - order
        basis = jnp.exp(-(arg * arg))
        ddist = jnp.sum(dbasis * basis * arg, axis=0, keepdims=True)
        for q, row in enumerate([ddist, denv] + spread_rows[1:]):
            grad[q, pl.ds(g, 1), :] += row

    w3wide = []
    for t in range(2):
        hi, low = hi_lo(w_in[t])
        w3wide.append(jnp.concatenate([hi, hi, low, low], axis=1).astype(BF16))

    grad[...] = jnp.zeros_like(grad)
    acc[...] = jnp.zeros_like(acc)

    arrive(send_one)
    gather_table(tab1)

    def first(g):
        radial(0, g)
        messages(0, g)

    groups(first)
    z_one = mixed(0)

    def own_rows(table, cx, cy):
        return table[1 + cx, 1 + cy].astype(F32)

    for cx in range(2):
        for cy in range(2):
            at = 16 * (2 * cx + cy)
            rows = z_one[at : at + 16] + own_rows(tab1, cx, cy)
            tab2[1 + cx, 1 + cy] = rows.astype(BF16)
    start(send_two)
    groups(functools.partial(radial, 1))

    arrive(send_two)
    gather_table(tab2)
    groups(functools.partial(messages, 1))
    z_two = mixed(1) + jnp.concatenate(
        [own_rows(tab2, cx, cy) for cx in range(2) for cy in range(2)], axis=0
    )
    sig = 0.5 * jnp.tanh(0.5 * z_two) + 0.5
    silu = z_two * sig
    out = jnp.broadcast_to(readout[...], (8, 128))
    z_grad = (sig + silu * (1.0 - sig)) * readout[...]
    unmixed(1, z_grad)
    groups(functools.partial(scatter, 1))

    def put_ghosts(target, full):
        for hx in range(4):
            for hy in range(4):
                if hx in (1, 2) and hy in (1, 2):
                    continue
                at = 16 * (4 * hx + hy)
                target[hx, hy] = full[at : at + 16].astype(target.dtype)

    full = scattered()
    put_ghosts(gs2, full)
    start(back_two)

    values = lax.dot_general(
        out, silu, (((1,), (1,)), ((), ())),
        precision=lax.Precision.HIGHEST, preferred_element_type=F32,
    )
    for cx in range(2):
        for cy in range(2):
            at = 16 * (2 * cx + cy)
            energy[cx, cy : cy + 1, :] = values[0:1, at : at + 16]

    def own_block(full):
        return jnp.concatenate(
            [full[16 * (4 * hx + hy) : 16 * (4 * hx + hy) + 16] for hx in (1, 2) for hy in (1, 2)],
            axis=0,
        )

    own_two = z_grad + own_block(full)
    acc[...] = jnp.zeros_like(acc)
    groups(functools.partial(coordinate_grads, 1))

    def returned(target, cx, cy):
        hx, hy = 3 * cx, 3 * cy
        return (
            target[hx, 1 + cy].astype(F32)
            + target[1 + cx, hy].astype(F32)
            + target[hx, hy].astype(F32)
        )

    arrive(back_two)
    own_two = own_two + jnp.concatenate(
        [returned(gr2, cx, cy) for cx in range(2) for cy in range(2)], axis=0
    )
    unmixed(0, own_two)
    groups(functools.partial(scatter, 0))
    full = scattered()
    put_ghosts(gs1, full)
    start(back_one)
    own_one = own_two + own_block(full)
    groups(functools.partial(coordinate_grads, 0))

    d = [grad[2 + m] for m in range(8)]
    ddist = grad[0] * (-2.0 / SPACING)
    dsq = ddist * (0.5 / distance) - grad[1] * (inside * live) * (2.0 / 36.0)
    du_x = d[0] + ROOT3 * (uy * d[3] + uz * d[6] + ux * d[7]) - ux * d[5]
    du_y = d[1] + ROOT3 * (ux * d[3] + uz * d[4] - uy * d[7]) - uy * d[5]
    du_z = d[2] + ROOT3 * (uy * d[4] + ux * d[6]) + 2.0 * uz * d[5]
    dsep = [
        2.0 * sep_x * dsq + du_x / 6.0,
        2.0 * sep_y * dsq + du_y / 6.0,
        2.0 * sep_z * dsq + du_z / 6.0,
    ]
    halves = [hi_lo(x) for x in dsep]
    total = jnp.zeros((16, 256), F32)
    blank = jnp.zeros((5, 256), F32)
    for g in range(GROUPS):
        rows = (
            [hi[g : g + 1] for hi, _ in halves] + [blank]
            + [low[g : g + 1] for _, low in halves] + [blank]
        )
        total = total + nt(jnp.concatenate(rows, axis=0).astype(BF16), oh[g])
    ghost_pos = total[0:8] + total[8:16]
    for hx in range(4):
        for hy in range(4):
            if hx in (1, 2) and hy in (1, 2):
                continue
            at = 16 * (4 * hx + hy)
            ps[hx, hy] = ghost_pos[0:3, at : at + 16]
    start(back_pos)

    stacked = jnp.concatenate([x for pair in halves for x in pair], axis=0).astype(BF16)
    narrow = nt(stacked, spread)
    mine = []
    for comp in range(3):
        at = 16 * comp
        mine.append((narrow[at : at + 8] + narrow[at + 8 : at + 16]) * half16)

    arrive(back_one)
    for cx in range(2):
        for cy in range(2):
            at = 16 * (2 * cx + cy)
            fgrad[cx, cy] = own_one[at : at + 16] + returned(gr1, cx, cy)

    arrive(back_pos)
    for cx in range(2):
        for cy in range(2):
            g = 2 * (2 * cx + cy)
            at = 16 * (4 * (1 + cx) + 1 + cy)
            given = jnp.concatenate([x[g : g + 1] + x[g + 1 : g + 2] for x in mine], axis=0)
            forces[cx, cy] = given - (ghost_pos[0:3, at : at + 16] + returned(pr, cx, cy))

    for group in (send_pos, send_one, send_two, back_two, back_one, back_pos):
        for copy in group:
            copy.wait_send()


def scratch():
    vmem = pltpu.VMEM
    return [
        vmem((4, 4, 16, 128), BF16),
        vmem((4, 4, 16, 128), BF16),
        vmem((4, 4, 3, 16), F32),
        vmem((4, 4, 16, 128), GRAD),
        vmem((4, 4, 16, 128), GRAD),
        vmem((4, 4, 16, 128), GRAD),
        vmem((4, 4, 16, 128), GRAD),
        vmem((4, 4, 3, 16), F32),
        vmem((4, 4, 3, 16), F32),
        vmem((8, 256, 256), BF16),
        vmem((8, 144, 256), BF16),
        vmem((11, 8, 256), F32),
        vmem((4, 8, 16), F32),
        vmem((8, 256), jnp.int32),
        vmem((2, 8, 64, 256), F32),
        vmem((2, 8, 64, 256), F32),
        vmem((2, 8, 384, 256), F32),
        vmem((2, 8, 384, 256), BF16),
        vmem((2, 8, 128, 256), F32),
        vmem((2, 8, 72, 128), F32),
        vmem((64, 384), F32),
        vmem((64, 384), F32),
        vmem((256, 256), F32),
        vmem((10, 8, 256), F32),
        vmem((2, 384, 256), BF16),
        vmem((2, 32, 64), BF16),
        vmem((2, 128, 384), BF16),
        vmem((2, 384, 256), BF16),
        vmem((128, 256), BF16),
        pltpu.SemaphoreType.DMA((6, 8)),
        pltpu.SemaphoreType.DMA((6, 8)),
    ]


def shards(nx, ny, features, positions, species, neighbours, counts, gain, w_in, w_out, mix, readout):
    shape = jax.ShapeDtypeStruct
    whole = pl.BlockSpec(memory_space=pltpu.VMEM)
    return pl.pallas_call(
        functools.partial(kernel, nx, ny),
        out_shape=(
            shape((2, 2, 16), F32),
            shape((2, 2, 3, 16), F32),
            shape((2, 2, 16, 128), F32),
        ),
        in_specs=[whole] * 10,
        out_specs=(whole,) * 3,
        scratch_shapes=scratch(),
        compiler_params=pltpu.CompilerParams(
            collective_id=0, has_side_effects=True, vmem_limit_bytes=50 * 1024 * 1024
        ),
        name="potential",
    )(
        features, positions, species, neighbours, counts, gain, w_in, w_out, mix,
        readout.reshape(1, -1),
    )


def solution(mesh):
    placed = (
        P("gx", "gy", None, None), P("gx", "gy", None, None), P("gx", "gy", None),
        P("gx", "gy", None, None), P("gx", "gy", None), P(), P(), P(), P(), P(),
    )
    return jax.shard_map(
        functools.partial(shards, mesh.shape["gx"], mesh.shape["gy"]),
        mesh=mesh,
        in_specs=placed,
        out_specs=(P("gx", "gy", None), P("gx", "gy", None, None), P("gx", "gy", None, None)),
        check_vma=False,
    )
```

```python
import functools

import jax
import jax.numpy as jnp
from jax import lax
from jax.experimental import pallas as pl
from jax.experimental.pallas import tpu as pltpu
from jax.sharding import PartitionSpec as P

F32 = jnp.float32
BF16 = jnp.bfloat16
MESH = pl.DeviceIdType.MESH
GRAD = BF16
DIRS = tuple((dx, dy) for dx in (-1, 0, 1) for dy in (-1, 0, 1) if (dx, dy) != (0, 0))
SPACING = 6.0 / 7.0
ROOT3 = 3.0**0.5
GROUPS = 8
PARTS = ((0, 8, 1, 0), (16, 24, 3, 1), (64, 40, 5, 4))


def nn(a, b):
    return lax.dot_general(a, b, (((1,), (0,)), ((), ())), preferred_element_type=F32)


def nt(a, b):
    return lax.dot_general(a, b, (((1,), (1,)), ((), ())), preferred_element_type=F32)


def tn(a, b):
    return lax.dot_general(a, b, (((0,), (0,)), ((), ())), preferred_element_type=F32)


def hi_lo(x):
    hi = x.astype(BF16).astype(F32)
    return hi, x - hi


def three(x):
    hi, rest = hi_lo(x)
    mid, low = hi_lo(rest)
    return hi, mid, low


def iota(shape, dim):
    return lax.broadcasted_iota(jnp.int32, shape, dim)


def kernel(
    nx, ny,
    feat_h, pos_h, spec_h, nb_h, cnt_h, gain_h, w_in_h, w_out_h, mix_h, readout_h,
    energy, forces, fgrad,
    feat, pos, spec, nb, cnt, gain, w_in, w_out, mix, readout,
    tab1, tab2, postab, gs2, gr2, gs1, gr1, ps, pr,
    oh, signed, amat, geo, atom, hid, dse, rad, pbf, pdf, xjt, msg, inv, dinv, dcat, frc,
    wo3, w3, mixc, tabt,
    lsem, ssem, rsem,
):
    gx, gy = lax.axis_index("gx"), lax.axis_index("gy")
    peers = [(lax.rem(gx + (dx + nx), nx), lax.rem(gy + (dy + ny), ny)) for dx, dy in DIRS]

    barrier = pltpu.get_barrier_semaphore()
    for peer in peers:
        pl.semaphore_signal(barrier, inc=1, device_id=peer, device_id_type=MESH)

    def pick(d, up, down, mid):
        return up if d == 1 else down if d == -1 else mid

    def copies(slot, src, dst, src_at, dst_at):
        out = []
        for k, (dx, dy) in enumerate(DIRS):
            out.append(
                pltpu.make_async_remote_copy(
                    src_ref=src.at[src_at(dx), src_at(dy)],
                    dst_ref=dst.at[dst_at(dx), dst_at(dy)],
                    send_sem=ssem.at[slot, k],
                    recv_sem=rsem.at[slot, k],
                    device_id=peers[k],
                    device_id_type=MESH,
                )
            )
        return out

    centre = pl.ds(1, 2)

    def owned_at(d):
        return pick(d, 2, 1, centre)

    def halo_at(d):
        return pick(d, 0, 3, centre)

    def ghost_at(d):
        return pick(d, 3, 0, centre)

    send_pos = copies(0, postab, postab, owned_at, halo_at)
    send_one = copies(1, tab1, tab1, owned_at, halo_at)
    send_two = copies(2, tab2, tab2, owned_at, halo_at)
    back_two = copies(3, gs2, gr2, ghost_at, halo_at)
    back_one = copies(4, gs1, gr1, ghost_at, halo_at)
    back_pos = copies(5, ps, pr, ghost_at, halo_at)

    def start(group):
        for copy in group:
            copy.start()

    def arrive(group):
        for copy in group:
            copy.wait_recv()

    sources = (pos_h, spec_h, feat_h, gain_h, nb_h, cnt_h, w_in_h, w_out_h, mix_h, readout_h)
    targets = (pos, spec, feat, gain, nb, cnt, w_in, w_out, mix, readout)
    loads = [
        pltpu.make_async_copy(source, target, lsem.at[k])
        for k, (source, target) in enumerate(zip(sources, targets))
    ]
    start(loads)

    loads[0].wait()
    for cx in range(2):
        for cy in range(2):
            for comp in range(3):
                postab[1 + cx, 1 + cy, comp : comp + 1, :] = pos[cx, comp, cy : cy + 1, :]
    for k in (1, 2, 3):
        loads[k].wait()
    kinds = gain.shape[0]
    for cx in range(2):
        for cy in range(2):
            onehot = (iota((kinds, 16), 0) == spec[cx, cy : cy + 1, :]).astype(F32)
            rows = lax.dot_general(
                onehot, gain[...], (((0,), (0,)), ((), ())),
                precision=lax.Precision.HIGHEST, preferred_element_type=F32,
            )
            tab1[1 + cx, 1 + cy] = (feat[cx, cy].astype(F32) * rows).astype(BF16)

    pl.semaphore_wait(barrier, len(DIRS))
    start(send_pos)
    start(send_one)

    for k in (4, 5):
        loads[k].wait()
    sub = iota((8, 256), 0)
    lane = iota((8, 256), 1)
    lane_atom = lax.shift_right_logical(lane, 5)
    diag = (sub == lane_atom).astype(F32)
    codes = nb[...].reshape(64, 32).astype(F32).astype(BF16)
    tile = (iota((32, 256), 0) == (iota((32, 256), 1) & 31)).astype(BF16)
    repeated = nn(codes, tile)
    keep = (iota((64, 256), 0) & 7) == lax.shift_right_logical(iota((64, 256), 1), 5)
    repeated = jnp.where(keep, repeated, 0.0).astype(BF16)
    gather8 = (iota((8, 64), 0) == lax.shift_right_logical(iota((8, 64), 1), 3)).astype(BF16)
    code = nn(gather8, repeated).astype(jnp.int32)
    offset = lax.shift_right_logical(code, 4)
    step_x = (offset >= 3).astype(jnp.int32) + (offset >= 6).astype(jnp.int32)
    step_y = offset - 3 * step_x
    halo_x = lax.shift_right_logical(sub, 2) + step_x
    halo_y = (lax.shift_right_logical(sub, 1) & 1) + step_y
    index = (halo_x * 4 + halo_y) * 16 + (code & 15)

    for g in range(GROUPS):
        atom[g : g + 1, :] = cnt[g // 4, g // 2 % 2 : g // 2 % 2 + 1, :].astype(F32)
    half16 = lax.shift_right_logical(iota((8, 16), 1), 3) == (iota((8, 16), 0) & 1)
    spread = (
        (iota((16, 256), 0) & 7) == lax.shift_right_logical(iota((16, 256), 1), 5)
    ).astype(BF16)
    count = nn(jnp.where(half16, atom[...], 0.0).astype(BF16), spread)
    live = ((lane & 31).astype(F32) < count).astype(F32)

    def at(g):
        return slice(256 * g, 256 * g + 256)

    candidate = iota((256, 256), 0)
    for g in range(GROUPS):
        found = (candidate == index[g : g + 1]).astype(F32)
        oh[:, at(g)] = found.astype(BF16)
        mine = 16 * (4 * (1 + g // 4) + 1 + g // 2 % 2) + 8 * (g % 2)
        signed[:, at(g)] = jnp.concatenate(
            [found[:mine], found[mine : mine + 8] - diag, found[mine + 8 :]], axis=0
        ).astype(BF16)

    for k in (6, 7, 8, 9):
        loads[k].wait()
    for t in range(2):
        hi, low = hi_lo(w_out[t])
        wo3[t] = jnp.concatenate([hi, hi, low, low], axis=0).T.astype(BF16)
        hi, low = hi_lo(w_in[t])
        w3[t] = jnp.concatenate([hi, hi, low, low], axis=0).astype(BF16)
        hi, low = hi_lo(mix[t])
        mixc[t] = jnp.concatenate([hi, low], axis=1).astype(BF16)

    arrive(send_pos)
    spots = [postab[hx, hy] for hx in range(4) for hy in range(4)]
    lanes = jnp.concatenate(spots, axis=1)
    lanes = jnp.concatenate([lanes, jnp.zeros((5, 256), F32)], axis=0)
    split = jnp.concatenate(list(three(lanes)) + [jnp.zeros((8, 256), F32)], axis=0).astype(BF16)
    for g in range(GROUPS):
        found = nn(split, signed[:, at(g)])
        found = found[0:8] + (found[8:16] + found[16:24])
        for comp in range(3):
            geo[comp, g : g + 1, :] = found[comp : comp + 1]
    ux = geo[0] / 6.0 + (step_x - 1).astype(F32)
    uy = geo[1] / 6.0 + (step_y - 1).astype(F32)
    uz = geo[2] / 6.0
    unit_sq = ux * ux + uy * uy + uz * uz
    distance = jnp.sqrt(36.0 * unit_sq + 0.01)
    inside = jnp.maximum(1.0 - unit_sq, 0.0)
    inside_live = inside * live
    geo[0] = ux
    geo[1] = uy
    geo[2] = uz
    geo[3] = ROOT3 * ux * uy
    geo[4] = ROOT3 * uy * uz
    geo[5] = uz * uz - 0.5 * (ux * ux + uy * uy)
    geo[6] = ROOT3 * ux * uz
    geo[7] = 0.5 * ROOT3 * (ux * ux - uy * uy)
    geo[8] = distance / SPACING
    geo[9] = inside * inside_live
    geo[10] = -1.0 / (SPACING * distance)
    geo[11] = (-2.0 / 36.0) * inside_live

    def row(q, g):
        return geo[q, g : g + 1, :]

    order = iota((8, 256), 0).astype(F32)

    def four_basis(x):
        hi, low = hi_lo(x)
        return jnp.concatenate([hi, low, hi, low], axis=0).astype(BF16)

    def radial(t, g):
        arg = row(8, g) - order
        envelope = row(9, g)
        pre = tn(w3[t], four_basis(jnp.exp(-(arg * arg))))
        sig = 0.5 * jnp.tanh(0.5 * pre) + 0.5
        silu = pre * sig
        hid[t, g] = silu
        dse[t, g] = (sig + silu * (1.0 - sig)) * envelope
        rad[t, g] = nn(wo3[t], four_basis(silu * envelope))

    def radial_grad(t, g):
        arg = row(8, g) - order
        dpre = tn(w3[t], four_basis(jnp.exp(-(arg * arg)) * arg * row(10, g)))
        change = nn(wo3[t], four_basis(dse[t, g] * dpre + hid[t, g] * row(11, g)))
        found = xjt[t, g]
        for part in range(3):
            lines = slice(128 * part, 128 * part + 128)
            pdf[t, g, lines, :] = (change[lines] * found).astype(BF16)

    def make_harmonics(g):
        rows = []
        for _, _, parts, first in PARTS:
            split_rows = [
                hi_lo(row(first + m - 1, g) * diag) if first else (diag, jnp.zeros_like(diag))
                for m in range(parts)
            ]
            rows += [hi for hi, _ in split_rows] + [low for _, low in split_rows]
        amat[g] = jnp.concatenate(rows, axis=0).astype(BF16)

    def groups(body, *args):
        for g in range(GROUPS):
            body(*args, g)

    groups(radial, 0)
    groups(make_harmonics)

    def gather_table(table):
        tabt[...] = table[...].reshape(256, 128).astype(F32).T.astype(BF16)

    def messages(t, g):
        found = nn(tabt[...], oh[:, at(g)])
        xjt[t, g] = found
        for part, (begin, rows, parts, first) in enumerate(PARTS):
            lines = slice(128 * part, 128 * part + 128)
            prod = (rad[t, g, lines, :] * found).astype(BF16)
            pbf[t, g, lines, :] = prod
            both = nt(amat[g, begin : begin + 2 * rows, :], prod)
            got = both[:rows] + both[rows:]
            msg[t, g, 8 * first : 8 * first + rows, :] = got
            if part == 0:
                total = got
            else:
                square = got * got
                total = square[0:8]
                for m in range(1, parts):
                    total = total + square[8 * m : 8 * m + 8]
            inv[8 * g : 8 * g + 8, lines] = total

    def mixed(t):
        hi, low = hi_lo(inv[...])
        both = nn(jnp.concatenate([hi, low], axis=0).astype(BF16), mixc[t])
        return (both[64:, :128] + both[:64, 128:]) + both[:64, :128]

    def unmixed(t, cotangent):
        hi, low = hi_lo(cotangent)
        left = jnp.concatenate(
            [jnp.concatenate([hi, hi], axis=1), jnp.concatenate([low, low], axis=1)], axis=0
        ).astype(BF16)
        both = nt(left, mixc[t])
        dinv[...] = both[:64] + both[64:]

    def message_grads(t, g, part):
        begin, rows, parts, first = PARTS[part]
        base = dinv[8 * g : 8 * g + 8, 128 * part : 128 * part + 128]
        if part == 0:
            return base
        base = base + base
        return jnp.concatenate(
            [msg[t, g, 8 * (first + m) : 8 * (first + m) + 8, :] * base for m in range(parts)],
            axis=0,
        )

    def feature_grads(t, g):
        total = None
        for part, (begin, rows, parts, first) in enumerate(PARTS):
            got = message_grads(t, g, part)
            dp = tn(
                jnp.concatenate([got, got], axis=0).astype(BF16), amat[g, begin : begin + 2 * rows, :]
            )
            term = dp * rad[t, g, 128 * part : 128 * part + 128, :]
            total = term if total is None else total + term
        hi, low = hi_lo(total)
        dcat[:, at(g)] = jnp.concatenate([hi, low], axis=0).astype(BF16)

    def scattered():
        both = nt(oh[...], dcat[...])
        return both[:, :128] + both[:, 128:]

    def separation_grads(t, g):
        plain, change = [], None
        for part, (begin, rows, parts, first) in enumerate(PARTS):
            lines = slice(128 * part, 128 * part + 128)
            hi, low = hi_lo(message_grads(t, g, part))
            left = jnp.concatenate([hi, low], axis=0).astype(BF16)
            if part:
                both = nn(left, pbf[t, g, lines, :])
                both = both[:rows] + both[rows:]
                plain += [both[8 * m : 8 * m + 8] for m in range(parts)]
            both = nn(left, pdf[t, g, lines, :])
            both = both[:rows] + both[rows:]
            for m in range(parts):
                term = both[8 * m : 8 * m + 8]
                if part:
                    term = term * row(first + m - 1, g)
                change = term if change is None else change + term
        d = plain
        ax, ay, az = row(0, g), row(1, g), row(2, g)
        change = 72.0 * change
        fx = d[0] + ROOT3 * (ay * d[3] + az * d[6] + ax * d[7]) + ax * (change - d[5])
        fy = d[1] + ROOT3 * (ax * d[3] + az * d[4] - ay * d[7]) + ay * (change - d[5])
        fz = d[2] + ROOT3 * (ay * d[4] + ax * d[6]) + az * (change + 2.0 * d[5])
        whole = jnp.concatenate([fx * diag, fy * diag, fz * diag], axis=0)
        if t == 1:
            frc[:, at(g)] = whole
        else:
            frc[:, at(g)] += whole

    arrive(send_one)
    gather_table(tab1)
    groups(messages, 0)
    z_one = mixed(0)

    def own_rows(table, cx, cy):
        return table[1 + cx, 1 + cy].astype(F32)

    for cx in range(2):
        for cy in range(2):
            first = 16 * (2 * cx + cy)
            rows = z_one[first : first + 16] + own_rows(tab1, cx, cy)
            tab2[1 + cx, 1 + cy] = rows.astype(BF16)
    start(send_two)
    groups(radial, 1)
    groups(radial_grad, 0)

    arrive(send_two)
    gather_table(tab2)
    groups(messages, 1)
    z_two = mixed(1) + jnp.concatenate(
        [own_rows(tab2, cx, cy) for cx in range(2) for cy in range(2)], axis=0
    )
    sig = 0.5 * jnp.tanh(0.5 * z_two) + 0.5
    silu = z_two * sig
    out = jnp.broadcast_to(readout[...], (8, 128))
    z_grad = (sig + silu * (1.0 - sig)) * readout[...]
    unmixed(1, z_grad)
    groups(feature_grads, 1)

    def put_ghosts(target, full):
        for hx in range(4):
            for hy in range(4):
                if hx in (1, 2) and hy in (1, 2):
                    continue
                first = 16 * (4 * hx + hy)
                target[hx, hy] = full[first : first + 16].astype(target.dtype)

    full = scattered()
    put_ghosts(gs2, full)
    start(back_two)

    values = lax.dot_general(
        out, silu, (((1,), (1,)), ((), ())),
        precision=lax.Precision.HIGHEST, preferred_element_type=F32,
    )
    for cx in range(2):
        for cy in range(2):
            first = 16 * (2 * cx + cy)
            energy[cx, cy : cy + 1, :] = values[0:1, first : first + 16]

    def own_block(full):
        return jnp.concatenate(
            [full[16 * (4 * hx + hy) : 16 * (4 * hx + hy) + 16] for hx in (1, 2) for hy in (1, 2)],
            axis=0,
        )

    own_two = z_grad + own_block(full)
    groups(radial_grad, 1)
    groups(separation_grads, 1)

    def returned(target, cx, cy):
        hx, hy = 3 * cx, 3 * cy
        return (
            target[hx, 1 + cy].astype(F32)
            + target[1 + cx, hy].astype(F32)
            + target[hx, hy].astype(F32)
        )

    arrive(back_two)
    own_two = own_two + jnp.concatenate(
        [returned(gr2, cx, cy) for cx in range(2) for cy in range(2)], axis=0
    )
    unmixed(0, own_two)
    groups(feature_grads, 0)
    full = scattered()
    put_ghosts(gs1, full)
    start(back_one)
    own_one = own_two + own_block(full)
    groups(separation_grads, 0)

    hi, low = hi_lo(frc[...])
    both = nt(jnp.concatenate([hi, low], axis=0).astype(BF16), signed[...])
    both = both[:24] + both[24:]
    moved = jnp.concatenate(
        [jnp.sum(both[8 * c : 8 * c + 8], axis=0, keepdims=True) for c in range(3)], axis=0
    ) * (1.0 / 6.0)
    for hx in range(4):
        for hy in range(4):
            if hx in (1, 2) and hy in (1, 2):
                continue
            first = 16 * (4 * hx + hy)
            ps[hx, hy] = moved[:, first : first + 16]
    start(back_pos)

    arrive(back_one)
    for cx in range(2):
        for cy in range(2):
            first = 16 * (2 * cx + cy)
            fgrad[cx, cy] = own_one[first : first + 16] + returned(gr1, cx, cy)

    arrive(back_pos)
    for cx in range(2):
        for cy in range(2):
            first = 16 * (4 * (1 + cx) + 1 + cy)
            total = -(moved[:, first : first + 16] + returned(pr, cx, cy))
            for comp in range(3):
                forces[cx, comp, cy : cy + 1, :] = total[comp : comp + 1]

    for group in (send_pos, send_one, send_two, back_two, back_one, back_pos):
        for copy in group:
            copy.wait_send()


def scratch():
    vmem = pltpu.VMEM
    return [
        vmem((2, 2, 16, 128), BF16),
        vmem((2, 3, 2, 16), F32),
        vmem((2, 2, 16), jnp.int32),
        vmem((2, 2, 16, 32), jnp.int32),
        vmem((2, 2, 16), jnp.int32),
        vmem((6, 128), F32),
        vmem((2, 8, 64), F32),
        vmem((2, 64, 384), F32),
        vmem((2, 384, 128), F32),
        vmem((1, 128), F32),
        vmem((4, 4, 16, 128), BF16),
        vmem((4, 4, 16, 128), BF16),
        vmem((4, 4, 3, 16), F32),
        vmem((4, 4, 16, 128), GRAD),
        vmem((4, 4, 16, 128), GRAD),
        vmem((4, 4, 16, 128), GRAD),
        vmem((4, 4, 16, 128), GRAD),
        vmem((4, 4, 3, 16), F32),
        vmem((4, 4, 3, 16), F32),
        vmem((256, 2048), BF16),
        vmem((256, 2048), BF16),
        vmem((8, 144, 256), BF16),
        vmem((12, 8, 256), F32),
        vmem((8, 16), F32),
        vmem((2, 8, 64, 256), F32),
        vmem((2, 8, 64, 256), F32),
        vmem((2, 8, 384, 256), F32),
        vmem((2, 8, 384, 256), BF16),
        vmem((2, 8, 384, 256), BF16),
        vmem((2, 8, 128, 256), F32),
        vmem((2, 8, 72, 128), F32),
        vmem((64, 384), F32),
        vmem((64, 384), F32),
        vmem((256, 2048), BF16),
        vmem((24, 2048), F32),
        vmem((2, 384, 256), BF16),
        vmem((2, 32, 64), BF16),
        vmem((2, 384, 256), BF16),
        vmem((128, 256), BF16),
        pltpu.SemaphoreType.DMA((10,)),
        pltpu.SemaphoreType.DMA((6, 8)),
        pltpu.SemaphoreType.DMA((6, 8)),
    ]


def shards(nx, ny, features, positions, species, neighbours, counts, gain, w_in, w_out, mix, readout):
    shape = jax.ShapeDtypeStruct
    outside = pl.BlockSpec(memory_space=pl.ANY)
    whole = pl.BlockSpec(memory_space=pltpu.VMEM)
    energy, forces, fgrad = pl.pallas_call(
        functools.partial(kernel, nx, ny),
        out_shape=(
            shape((2, 2, 16), F32),
            shape((2, 3, 2, 16), F32),
            shape((2, 2, 16, 128), F32),
        ),
        in_specs=[outside] * 10,
        out_specs=(whole,) * 3,
        scratch_shapes=scratch(),
        compiler_params=pltpu.CompilerParams(
            collective_id=0, has_side_effects=True, vmem_limit_bytes=60 * 1024 * 1024
        ),
        name="potential",
    )(
        features, jnp.transpose(positions, (0, 2, 1, 3)), species, neighbours, counts, gain,
        w_in, w_out, mix, readout.reshape(1, -1),
    )
    return energy, jnp.transpose(forces, (0, 2, 1, 3)), fgrad


def solution(mesh):
    placed = (
        P("gx", "gy", None, None), P("gx", "gy", None, None), P("gx", "gy", None),
        P("gx", "gy", None, None), P("gx", "gy", None), P(), P(), P(), P(), P(),
    )
    return jax.shard_map(
        functools.partial(shards, mesh.shape["gx"], mesh.shape["gy"]),
        mesh=mesh,
        in_specs=placed,
        out_specs=(P("gx", "gy", None), P("gx", "gy", None, None), P("gx", "gy", None, None)),
        check_vma=False,
    )
```

```python
import functools

import jax
import jax.numpy as jnp
from jax import lax
from jax.experimental import pallas as pl
from jax.experimental.pallas import tpu as pltpu
from jax.sharding import PartitionSpec as P

F32 = jnp.float32
BF16 = jnp.bfloat16
MESH = pl.DeviceIdType.MESH
GRAD = BF16
DIRS = tuple((dx, dy) for dx in (-1, 0, 1) for dy in (-1, 0, 1) if (dx, dy) != (0, 0))
VLIM = 60
SPACING = 6.0 / 7.0
ROOT3 = 3.0**0.5
GROUPS = 8
PARTS = ((0, 8, 1, 0), (16, 24, 3, 1), (64, 40, 5, 4))


def nn(a, b):
    return lax.dot_general(a, b, (((1,), (0,)), ((), ())), preferred_element_type=F32)


def nt(a, b):
    return lax.dot_general(a, b, (((1,), (1,)), ((), ())), preferred_element_type=F32)


def tn(a, b):
    return lax.dot_general(a, b, (((0,), (0,)), ((), ())), preferred_element_type=F32)


def hi_lo(x):
    hi = x.astype(BF16).astype(F32)
    return hi, x - hi


def three(x):
    hi, rest = hi_lo(x)
    mid, low = hi_lo(rest)
    return hi, mid, low


def iota(shape, dim):
    return lax.broadcasted_iota(jnp.int32, shape, dim)


def kernel(
    nx, ny,
    feat_h, pos_h, spec_h, nb_h, cnt_h, gain_h, w_in_h, w_out_h, mix_h, readout_h,
    energy, forces, fgrad,
    feat, pos, spec, nb, cnt, gain, w_in, w_out, mix, readout,
    tab1, tab2, postab, gs2, gr2, gs1, gr1, ps, pr,
    oh, signed, amat, geo, atom, hid, dse, rad, pbf, pdf, xjt, msg, inv, dinv, dcat, frc,
    wo3, w3, mixc, tabt,
    lsem, ssem, rsem,
):
    gx, gy = lax.axis_index("gx"), lax.axis_index("gy")
    peers = [(lax.rem(gx + (dx + nx), nx), lax.rem(gy + (dy + ny), ny)) for dx, dy in DIRS]

    barrier = pltpu.get_barrier_semaphore()
    for peer in peers:
        pl.semaphore_signal(barrier, inc=1, device_id=peer, device_id_type=MESH)

    def pick(d, up, down, mid):
        return up if d == 1 else down if d == -1 else mid

    def copies(slot, src, dst, src_at, dst_at):
        out = []
        for k, (dx, dy) in enumerate(DIRS):
            out.append(
                pltpu.make_async_remote_copy(
                    src_ref=src.at[src_at(dx), src_at(dy)],
                    dst_ref=dst.at[dst_at(dx), dst_at(dy)],
                    send_sem=ssem.at[slot, k],
                    recv_sem=rsem.at[slot, k],
                    device_id=peers[k],
                    device_id_type=MESH,
                )
            )
        return out

    centre = pl.ds(1, 2)

    def owned_at(d):
        return pick(d, 2, 1, centre)

    def halo_at(d):
        return pick(d, 0, 3, centre)

    def ghost_at(d):
        return pick(d, 3, 0, centre)

    send_pos = copies(0, postab, postab, owned_at, halo_at)
    send_one = copies(1, tab1, tab1, owned_at, halo_at)
    send_two = copies(2, tab2, tab2, owned_at, halo_at)
    back_two = copies(3, gs2, gr2, ghost_at, halo_at)
    back_one = copies(4, gs1, gr1, ghost_at, halo_at)
    back_pos = copies(5, ps, pr, ghost_at, halo_at)

    def start(group):
        for copy in group:
            copy.start()

    def arrive(group):
        for copy in group:
            copy.wait_recv()

    sources = (pos_h, spec_h, feat_h, gain_h, nb_h, cnt_h, w_in_h, w_out_h, mix_h, readout_h)
    targets = (pos, spec, feat, gain, nb, cnt, w_in, w_out, mix, readout)
    loads = [
        pltpu.make_async_copy(source, target, lsem.at[k])
        for k, (source, target) in enumerate(zip(sources, targets))
    ]
    start(loads)

    loads[0].wait()
    for cx in range(2):
        for cy in range(2):
            for comp in range(3):
                postab[1 + cx, 1 + cy, comp : comp + 1, :] = pos[cx, comp, cy : cy + 1, :]
    for k in (1, 2, 3):
        loads[k].wait()
    kinds = gain.shape[0]
    for cx in range(2):
        for cy in range(2):
            onehot = (iota((kinds, 16), 0) == spec[cx, cy : cy + 1, :]).astype(F32)
            rows = lax.dot_general(
                onehot, gain[...], (((0,), (0,)), ((), ())),
                precision=lax.Precision.HIGHEST, preferred_element_type=F32,
            )
            tab1[1 + cx, 1 + cy] = (feat[cx, cy].astype(F32) * rows).astype(BF16)

    pl.semaphore_wait(barrier, len(DIRS))
    start(send_pos)
    start(send_one)

    for k in (4, 5):
        loads[k].wait()
    sub = iota((8, 256), 0)
    lane = iota((8, 256), 1)
    lane_atom = lax.shift_right_logical(lane, 5)
    diag = (sub == lane_atom).astype(F32)
    codes = nb[...].reshape(64, 32).astype(F32).astype(BF16)
    tile = (iota((32, 256), 0) == (iota((32, 256), 1) & 31)).astype(BF16)
    repeated = nn(codes, tile)
    keep = (iota((64, 256), 0) & 7) == lax.shift_right_logical(iota((64, 256), 1), 5)
    repeated = jnp.where(keep, repeated, 0.0).astype(BF16)
    gather8 = (iota((8, 64), 0) == lax.shift_right_logical(iota((8, 64), 1), 3)).astype(BF16)
    code = nn(gather8, repeated).astype(jnp.int32)
    offset = lax.shift_right_logical(code, 4)
    step_x = (offset >= 3).astype(jnp.int32) + (offset >= 6).astype(jnp.int32)
    step_y = offset - 3 * step_x
    halo_x = lax.shift_right_logical(sub, 2) + step_x
    halo_y = (lax.shift_right_logical(sub, 1) & 1) + step_y
    index = (halo_x * 4 + halo_y) * 16 + (code & 15)

    for g in range(GROUPS):
        atom[g : g + 1, :] = cnt[g // 4, g // 2 % 2 : g // 2 % 2 + 1, :].astype(F32)
    half16 = lax.shift_right_logical(iota((8, 16), 1), 3) == (iota((8, 16), 0) & 1)
    spread = (
        (iota((16, 256), 0) & 7) == lax.shift_right_logical(iota((16, 256), 1), 5)
    ).astype(BF16)
    count = nn(jnp.where(half16, atom[...], 0.0).astype(BF16), spread)
    live = ((lane & 31).astype(F32) < count).astype(F32)

    def at(g):
        return slice(256 * g, 256 * g + 256)

    candidate = iota((256, 256), 0)
    for g in range(GROUPS):
        found = (candidate == index[g : g + 1]).astype(F32)
        oh[:, at(g)] = found.astype(BF16)
        mine = 16 * (4 * (1 + g // 4) + 1 + g // 2 % 2) + 8 * (g % 2)
        signed[:, at(g)] = jnp.concatenate(
            [found[:mine], found[mine : mine + 8] - diag, found[mine + 8 :]], axis=0
        ).astype(BF16)

    for k in (6, 7, 8, 9):
        loads[k].wait()
    for t in range(2):
        hi, low = hi_lo(w_out[t])
        wo3[t] = jnp.concatenate([hi, hi, low, low], axis=0).T.astype(BF16)
        hi, low = hi_lo(w_in[t])
        w3[t] = jnp.concatenate([hi, hi, low, low], axis=0).astype(BF16)
        hi, low = hi_lo(mix[t])
        mixc[t] = jnp.concatenate([hi, low], axis=1).astype(BF16)

    arrive(send_pos)
    spots = [postab[hx, hy] for hx in range(4) for hy in range(4)]
    lanes = jnp.concatenate(spots, axis=1)
    lanes = jnp.concatenate([lanes, jnp.zeros((5, 256), F32)], axis=0)
    split = jnp.concatenate(list(three(lanes)) + [jnp.zeros((8, 256), F32)], axis=0).astype(BF16)
    for g in range(GROUPS):
        found = nn(split, signed[:, at(g)])
        found = found[0:8] + (found[8:16] + found[16:24])
        for comp in range(3):
            geo[comp, g : g + 1, :] = found[comp : comp + 1]
    ux = geo[0] / 6.0 + (step_x - 1).astype(F32)
    uy = geo[1] / 6.0 + (step_y - 1).astype(F32)
    uz = geo[2] / 6.0
    unit_sq = ux * ux + uy * uy + uz * uz
    distance = jnp.sqrt(36.0 * unit_sq + 0.01)
    inside = jnp.maximum(1.0 - unit_sq, 0.0)
    inside_live = inside * live
    geo[0] = ux
    geo[1] = uy
    geo[2] = uz
    geo[3] = ROOT3 * ux * uy
    geo[4] = ROOT3 * uy * uz
    geo[5] = uz * uz - 0.5 * (ux * ux + uy * uy)
    geo[6] = ROOT3 * ux * uz
    geo[7] = 0.5 * ROOT3 * (ux * ux - uy * uy)
    geo[8] = distance / SPACING
    geo[9] = inside * inside_live
    geo[10] = -1.0 / (SPACING * distance)
    geo[11] = (-2.0 / 36.0) * inside_live

    def row(q, g):
        return geo[q, g : g + 1, :]

    order = iota((8, 256), 0).astype(F32)

    def four_basis(x):
        hi, low = hi_lo(x)
        return jnp.concatenate([hi, low, hi, low], axis=0).astype(BF16)

    def radial(t, g):
        arg = row(8, g) - order
        envelope = row(9, g)
        pre = tn(w3[t], four_basis(jnp.exp(-(arg * arg))))
        sig = 0.5 * jnp.tanh(0.5 * pre) + 0.5
        silu = pre * sig
        hid[t, g] = silu
        dse[t, g] = (sig + silu * (1.0 - sig)) * envelope
        rad[t, g] = nn(wo3[t], four_basis(silu * envelope))

    def radial_grad(t, g):
        arg = row(8, g) - order
        dpre = tn(w3[t], four_basis(jnp.exp(-(arg * arg)) * arg * row(10, g)))
        change = nn(wo3[t], four_basis(dse[t, g] * dpre + hid[t, g] * row(11, g)))
        found = xjt[t, g]
        for part in range(3):
            lines = slice(128 * part, 128 * part + 128)
            pdf[t, g, lines, :] = (change[lines] * found).astype(BF16)

    def make_harmonics(g):
        rows = []
        for _, _, parts, first in PARTS:
            split_rows = [
                hi_lo(row(first + m - 1, g) * diag) if first else (diag, jnp.zeros_like(diag))
                for m in range(parts)
            ]
            rows += [hi for hi, _ in split_rows] + [low for _, low in split_rows]
        amat[g] = jnp.concatenate(rows, axis=0).astype(BF16)

    def groups(body, *args):
        for g in range(GROUPS):
            body(*args, g)

    groups(radial, 0)
    groups(make_harmonics)

    def gather_table(table):
        tabt[...] = table[...].reshape(256, 128).astype(F32).T.astype(BF16)

    def messages(t, g):
        found = nn(tabt[...], oh[:, at(g)])
        xjt[t, g] = found
        for part, (begin, rows, parts, first) in enumerate(PARTS):
            lines = slice(128 * part, 128 * part + 128)
            prod = (rad[t, g, lines, :] * found).astype(BF16)
            pbf[t, g, lines, :] = prod
            both = nt(amat[g, begin : begin + 2 * rows, :], prod)
            got = both[:rows] + both[rows:]
            msg[t, g, 8 * first : 8 * first + rows, :] = got
            if part == 0:
                total = got
            else:
                square = got * got
                total = square[0:8]
                for m in range(1, parts):
                    total = total + square[8 * m : 8 * m + 8]
            inv[8 * g : 8 * g + 8, lines] = total

    def mixed(t):
        hi, low = hi_lo(inv[...])
        both = nn(jnp.concatenate([hi, low], axis=0).astype(BF16), mixc[t])
        return (both[64:, :128] + both[:64, 128:]) + both[:64, :128]

    def unmixed(t, cotangent):
        hi, low = hi_lo(cotangent)
        left = jnp.concatenate(
            [jnp.concatenate([hi, hi], axis=1), jnp.concatenate([low, low], axis=1)], axis=0
        ).astype(BF16)
        both = nt(left, mixc[t])
        dinv[...] = both[:64] + both[64:]

    def message_grads(t, g, part):
        begin, rows, parts, first = PARTS[part]
        base = dinv[8 * g : 8 * g + 8, 128 * part : 128 * part + 128]
        if part == 0:
            return base
        base = base + base
        return jnp.concatenate(
            [msg[t, g, 8 * (first + m) : 8 * (first + m) + 8, :] * base for m in range(parts)],
            axis=0,
        )

    def feature_grads(t, g):
        total = None
        for part, (begin, rows, parts, first) in enumerate(PARTS):
            got = message_grads(t, g, part)
            dp = tn(
                jnp.concatenate([got, got], axis=0).astype(BF16), amat[g, begin : begin + 2 * rows, :]
            )
            term = dp * rad[t, g, 128 * part : 128 * part + 128, :]
            total = term if total is None else total + term
        hi, low = hi_lo(total)
        dcat[:, at(g)] = jnp.concatenate([hi, low], axis=0).astype(BF16)

    def scattered():
        both = nt(oh[...], dcat[...])
        return both[:, :128] + both[:, 128:]

    def separation_grads(t, g):
        plain, change = [], None
        for part, (begin, rows, parts, first) in enumerate(PARTS):
            lines = slice(128 * part, 128 * part + 128)
            hi, low = hi_lo(message_grads(t, g, part))
            left = jnp.concatenate([hi, low], axis=0).astype(BF16)
            if part:
                both = nn(left, pbf[t, g, lines, :])
                both = both[:rows] + both[rows:]
                plain += [both[8 * m : 8 * m + 8] for m in range(parts)]
            both = nn(left, pdf[t, g, lines, :])
            both = both[:rows] + both[rows:]
            for m in range(parts):
                term = both[8 * m : 8 * m + 8]
                if part:
                    term = term * row(first + m - 1, g)
                change = term if change is None else change + term
        d = plain
        ax, ay, az = row(0, g), row(1, g), row(2, g)
        change = 72.0 * change
        fx = d[0] + ROOT3 * (ay * d[3] + az * d[6] + ax * d[7]) + ax * (change - d[5])
        fy = d[1] + ROOT3 * (ax * d[3] + az * d[4] - ay * d[7]) + ay * (change - d[5])
        fz = d[2] + ROOT3 * (ay * d[4] + ax * d[6]) + az * (change + 2.0 * d[5])
        whole = jnp.concatenate([fx * diag, fy * diag, fz * diag], axis=0)
        if t == 1:
            frc[:, at(g)] = whole
        else:
            frc[:, at(g)] += whole

    arrive(send_one)
    gather_table(tab1)
    groups(messages, 0)
    z_one = mixed(0)

    def own_rows(table, cx, cy):
        return table[1 + cx, 1 + cy].astype(F32)

    for cx in range(2):
        for cy in range(2):
            first = 16 * (2 * cx + cy)
            rows = z_one[first : first + 16] + own_rows(tab1, cx, cy)
            tab2[1 + cx, 1 + cy] = rows.astype(BF16)
    start(send_two)
    groups(radial, 1)
    groups(radial_grad, 0)

    arrive(send_two)
    gather_table(tab2)
    groups(messages, 1)
    z_two = mixed(1) + jnp.concatenate(
        [own_rows(tab2, cx, cy) for cx in range(2) for cy in range(2)], axis=0
    )
    sig = 0.5 * jnp.tanh(0.5 * z_two) + 0.5
    silu = z_two * sig
    out = jnp.broadcast_to(readout[...], (8, 128))
    z_grad = (sig + silu * (1.0 - sig)) * readout[...]
    unmixed(1, z_grad)
    groups(feature_grads, 1)

    def put_ghosts(target, full):
        for hx in range(4):
            for hy in range(4):
                if hx in (1, 2) and hy in (1, 2):
                    continue
                first = 16 * (4 * hx + hy)
                target[hx, hy] = full[first : first + 16].astype(target.dtype)

    full = scattered()
    put_ghosts(gs2, full)
    start(back_two)

    values = lax.dot_general(
        out, silu, (((1,), (1,)), ((), ())),
        precision=lax.Precision.HIGHEST, preferred_element_type=F32,
    )
    for cx in range(2):
        for cy in range(2):
            first = 16 * (2 * cx + cy)
            energy[cx, cy : cy + 1, :] = values[0:1, first : first + 16]

    def own_block(full):
        return jnp.concatenate(
            [full[16 * (4 * hx + hy) : 16 * (4 * hx + hy) + 16] for hx in (1, 2) for hy in (1, 2)],
            axis=0,
        )

    own_two = z_grad + own_block(full)
    groups(radial_grad, 1)
    groups(separation_grads, 1)

    def returned(target, cx, cy):
        hx, hy = 3 * cx, 3 * cy
        return (
            target[hx, 1 + cy].astype(F32)
            + target[1 + cx, hy].astype(F32)
            + target[hx, hy].astype(F32)
        )

    arrive(back_two)
    own_two = own_two + jnp.concatenate(
        [returned(gr2, cx, cy) for cx in range(2) for cy in range(2)], axis=0
    )
    unmixed(0, own_two)
    groups(feature_grads, 0)
    full = scattered()
    put_ghosts(gs1, full)
    start(back_one)
    own_one = own_two + own_block(full)
    groups(separation_grads, 0)

    hi, low = hi_lo(frc[...])
    both = nt(jnp.concatenate([hi, low], axis=0).astype(BF16), signed[...])
    both = both[:24] + both[24:]
    moved = jnp.concatenate(
        [jnp.sum(both[8 * c : 8 * c + 8], axis=0, keepdims=True) for c in range(3)], axis=0
    ) * (1.0 / 6.0)
    for hx in range(4):
        for hy in range(4):
            if hx in (1, 2) and hy in (1, 2):
                continue
            first = 16 * (4 * hx + hy)
            ps[hx, hy] = moved[:, first : first + 16]
    start(back_pos)

    arrive(back_one)
    for cx in range(2):
        for cy in range(2):
            first = 16 * (2 * cx + cy)
            fgrad[cx, cy] = own_one[first : first + 16] + returned(gr1, cx, cy)

    arrive(back_pos)
    for cx in range(2):
        for cy in range(2):
            first = 16 * (4 * (1 + cx) + 1 + cy)
            total = -(moved[:, first : first + 16] + returned(pr, cx, cy))
            for comp in range(3):
                forces[cx, comp, cy : cy + 1, :] = total[comp : comp + 1]

    for group in (send_pos, send_one, send_two, back_two, back_one, back_pos):
        for copy in group:
            copy.wait_send()


def deliver(a, b, c, a_out, b_out, c_out, sem):
    moves = [
        pltpu.make_async_copy(source, target, sem.at[k])
        for k, (source, target) in enumerate(((a, a_out), (b, b_out), (c, c_out)))
    ]
    for move in moves:
        move.start()
    for move in moves:
        move.wait()


def scratch():
    vmem = pltpu.VMEM
    return [
        vmem((2, 2, 16, 128), BF16),
        vmem((2, 3, 2, 16), F32),
        vmem((2, 2, 16), jnp.int32),
        vmem((2, 2, 16, 32), jnp.int32),
        vmem((2, 2, 16), jnp.int32),
        vmem((6, 128), F32),
        vmem((2, 8, 64), F32),
        vmem((2, 64, 384), F32),
        vmem((2, 384, 128), F32),
        vmem((1, 128), F32),
        vmem((4, 4, 16, 128), BF16),
        vmem((4, 4, 16, 128), BF16),
        vmem((4, 4, 3, 16), F32),
        vmem((4, 4, 16, 128), GRAD),
        vmem((4, 4, 16, 128), GRAD),
        vmem((4, 4, 16, 128), GRAD),
        vmem((4, 4, 16, 128), GRAD),
        vmem((4, 4, 3, 16), F32),
        vmem((4, 4, 3, 16), F32),
        vmem((256, 2048), BF16),
        vmem((256, 2048), BF16),
        vmem((8, 144, 256), BF16),
        vmem((12, 8, 256), F32),
        vmem((8, 16), F32),
        vmem((2, 8, 64, 256), F32),
        vmem((2, 8, 64, 256), F32),
        vmem((2, 8, 384, 256), F32),
        vmem((2, 8, 384, 256), BF16),
        vmem((2, 8, 384, 256), BF16),
        vmem((2, 8, 128, 256), F32),
        vmem((2, 8, 72, 128), F32),
        vmem((64, 384), F32),
        vmem((64, 384), F32),
        vmem((256, 2048), BF16),
        vmem((24, 2048), F32),
        vmem((2, 384, 256), BF16),
        vmem((2, 32, 64), BF16),
        vmem((2, 384, 256), BF16),
        vmem((128, 256), BF16),
        pltpu.SemaphoreType.DMA((10,)),
        pltpu.SemaphoreType.DMA((6, 8)),
        pltpu.SemaphoreType.DMA((6, 8)),
    ]


def shards(nx, ny, features, positions, species, neighbours, counts, gain, w_in, w_out, mix, readout):
    shape = jax.ShapeDtypeStruct
    outside = pl.BlockSpec(memory_space=pl.ANY)
    whole = pl.BlockSpec(memory_space=pltpu.VMEM)
    energy, forces, fgrad = pl.pallas_call(
        functools.partial(kernel, nx, ny),
        out_shape=(
            pltpu.VMEM((2, 2, 16), F32),
            pltpu.VMEM((2, 3, 2, 16), F32),
            pltpu.VMEM((2, 2, 16, 128), F32),
        ),
        in_specs=[outside] * 10,
        out_specs=(whole,) * 3,
        scratch_shapes=scratch(),
        compiler_params=pltpu.CompilerParams(
            collective_id=0, has_side_effects=True, vmem_limit_bytes=VLIM * 1024 * 1024
        ),
        name="potential",
    )(
        features, jnp.transpose(positions, (0, 2, 1, 3)), species, neighbours, counts, gain,
        w_in, w_out, mix, readout.reshape(1, -1),
    )
    results = (energy, forces, fgrad)
    energy, forces, fgrad = pl.pallas_call(
        deliver,
        out_shape=tuple(shape(x.shape, x.dtype) for x in results),
        in_specs=[whole] * 3,
        out_specs=(pl.BlockSpec(memory_space=pltpu.HBM),) * 3,
        scratch_shapes=[pltpu.SemaphoreType.DMA((3,))],
        compiler_params=pltpu.CompilerParams(vmem_limit_bytes=1024 * 1024),
        name="deliver",
    )(*results)
    return energy, jnp.transpose(forces, (0, 2, 1, 3)), fgrad


def solution(mesh):
    placed = (
        P("gx", "gy", None, None), P("gx", "gy", None, None), P("gx", "gy", None),
        P("gx", "gy", None, None), P("gx", "gy", None), P(), P(), P(), P(), P(),
    )
    return jax.shard_map(
        functools.partial(shards, mesh.shape["gx"], mesh.shape["gy"]),
        mesh=mesh,
        in_specs=placed,
        out_specs=(P("gx", "gy", None), P("gx", "gy", None, None), P("gx", "gy", None, None)),
        check_vma=False,
    )
```

```python
import functools

import jax
import jax.numpy as jnp
from jax import lax
from jax.experimental import pallas as pl
from jax.experimental.pallas import tpu as pltpu
from jax.sharding import PartitionSpec as P

F32 = jnp.float32
BF16 = jnp.bfloat16
MESH = pl.DeviceIdType.MESH
GRAD = BF16
DIRS = tuple((dx, dy) for dx in (-1, 0, 1) for dy in (-1, 0, 1) if (dx, dy) != (0, 0))
VLIM = 60
SPACING = 6.0 / 7.0
ROOT3 = 3.0**0.5
GROUPS = 8
PARTS = ((0, 8, 1, 0), (16, 24, 3, 1), (48, 40, 5, 4))


def nn(a, b):
    return lax.dot_general(a, b, (((1,), (0,)), ((), ())), preferred_element_type=F32)


def nt(a, b):
    return lax.dot_general(a, b, (((1,), (1,)), ((), ())), preferred_element_type=F32)


def tn(a, b):
    return lax.dot_general(a, b, (((0,), (0,)), ((), ())), preferred_element_type=F32)


def hi_lo(x):
    hi = x.astype(BF16).astype(F32)
    return hi, x - hi


def three(x):
    hi, rest = hi_lo(x)
    mid, low = hi_lo(rest)
    return hi, mid, low


def iota(shape, dim):
    return lax.broadcasted_iota(jnp.int32, shape, dim)


def kernel(
    nx, ny,
    feat_h, pos_h, spec_h, nb_h, cnt_h, gain_h, w_in_h, w_out_h, mix_h, readout_h,
    energy, forces, fgrad,
    feat, pos, spec, nb, cnt, gain, w_in, w_out, mix, readout,
    tab1, tab2, postab, gs2, gr2, gs1, gr1, ps, pr,
    oh, signed, amat, geo, atom, hid, dse, rad, pbf, pdf, xjt, msg, inv, dinv, dcat, frc,
    wo3, w3, mixc, tabt,
    lsem, ssem, rsem,
):
    gx, gy = lax.axis_index("gx"), lax.axis_index("gy")
    peers = [(lax.rem(gx + (dx + nx), nx), lax.rem(gy + (dy + ny), ny)) for dx, dy in DIRS]

    barrier = pltpu.get_barrier_semaphore()
    for peer in peers:
        pl.semaphore_signal(barrier, inc=1, device_id=peer, device_id_type=MESH)

    def pick(d, up, down, mid):
        return up if d == 1 else down if d == -1 else mid

    def copies(slot, src, dst, src_at, dst_at):
        out = []
        for k, (dx, dy) in enumerate(DIRS):
            out.append(
                pltpu.make_async_remote_copy(
                    src_ref=src.at[src_at(dx), src_at(dy)],
                    dst_ref=dst.at[dst_at(dx), dst_at(dy)],
                    send_sem=ssem.at[slot, k],
                    recv_sem=rsem.at[slot, k],
                    device_id=peers[k],
                    device_id_type=MESH,
                )
            )
        return out

    centre = pl.ds(1, 2)

    def owned_at(d):
        return pick(d, 2, 1, centre)

    def halo_at(d):
        return pick(d, 0, 3, centre)

    def ghost_at(d):
        return pick(d, 3, 0, centre)

    send_pos = copies(0, postab, postab, owned_at, halo_at)
    send_one = copies(1, tab1, tab1, owned_at, halo_at)
    send_two = copies(2, tab2, tab2, owned_at, halo_at)
    back_two = copies(3, gs2, gr2, ghost_at, halo_at)
    back_one = copies(4, gs1, gr1, ghost_at, halo_at)
    back_pos = copies(5, ps, pr, ghost_at, halo_at)

    def start(group):
        for copy in group:
            copy.start()

    def arrive(group):
        for copy in group:
            copy.wait_recv()

    sources = (pos_h, spec_h, feat_h, gain_h, nb_h, cnt_h, w_in_h, w_out_h, mix_h, readout_h)
    targets = (pos, spec, feat, gain, nb, cnt, w_in, w_out, mix, readout)
    loads = [
        pltpu.make_async_copy(source, target, lsem.at[k])
        for k, (source, target) in enumerate(zip(sources, targets))
    ]
    start(loads)

    loads[0].wait()
    for cx in range(2):
        for cy in range(2):
            for comp in range(3):
                postab[1 + cx, 1 + cy, comp : comp + 1, :] = pos[cx, comp, cy : cy + 1, :]
    for k in (1, 2, 3):
        loads[k].wait()
    kinds = gain.shape[0]
    for cx in range(2):
        for cy in range(2):
            onehot = (iota((kinds, 16), 0) == spec[cx, cy : cy + 1, :]).astype(F32)
            rows = lax.dot_general(
                onehot, gain[...], (((0,), (0,)), ((), ())),
                precision=lax.Precision.HIGHEST, preferred_element_type=F32,
            )
            tab1[1 + cx, 1 + cy] = (feat[cx, cy].astype(F32) * rows).astype(BF16)

    pl.semaphore_wait(barrier, len(DIRS))
    start(send_pos)
    start(send_one)

    for k in (4, 5):
        loads[k].wait()
    sub = iota((8, 256), 0)
    lane = iota((8, 256), 1)
    lane_atom = lax.shift_right_logical(lane, 5)
    diag = (sub == lane_atom).astype(F32)
    codes = nb[...].reshape(64, 32).astype(F32).astype(BF16)
    tile = (iota((32, 256), 0) == (iota((32, 256), 1) & 31)).astype(BF16)
    repeated = nn(codes, tile)
    keep = (iota((64, 256), 0) & 7) == lax.shift_right_logical(iota((64, 256), 1), 5)
    repeated = jnp.where(keep, repeated, 0.0).astype(BF16)
    gather8 = (iota((8, 64), 0) == lax.shift_right_logical(iota((8, 64), 1), 3)).astype(BF16)
    code = nn(gather8, repeated).astype(jnp.int32)
    offset = lax.shift_right_logical(code, 4)
    step_x = (offset >= 3).astype(jnp.int32) + (offset >= 6).astype(jnp.int32)
    step_y = offset - 3 * step_x
    halo_x = lax.shift_right_logical(sub, 2) + step_x
    halo_y = (lax.shift_right_logical(sub, 1) & 1) + step_y
    index = (halo_x * 4 + halo_y) * 16 + (code & 15)

    for g in range(GROUPS):
        atom[g : g + 1, :] = cnt[g // 4, g // 2 % 2 : g // 2 % 2 + 1, :].astype(F32)
    half16 = lax.shift_right_logical(iota((8, 16), 1), 3) == (iota((8, 16), 0) & 1)
    spread = (
        (iota((16, 256), 0) & 7) == lax.shift_right_logical(iota((16, 256), 1), 5)
    ).astype(BF16)
    count = nn(jnp.where(half16, atom[...], 0.0).astype(BF16), spread)
    live = ((lane & 31).astype(F32) < count).astype(F32)

    def at(g):
        return slice(256 * g, 256 * g + 256)

    candidate = iota((256, 256), 0)
    for g in range(GROUPS):
        found = (candidate == index[g : g + 1]).astype(F32)
        oh[:, at(g)] = found.astype(BF16)
        mine = 16 * (4 * (1 + g // 4) + 1 + g // 2 % 2) + 8 * (g % 2)
        signed[:, at(g)] = jnp.concatenate(
            [found[:mine], found[mine : mine + 8] - diag, found[mine + 8 :]], axis=0
        ).astype(BF16)

    for k in (6, 7, 8, 9):
        loads[k].wait()
    for t in range(2):
        hi, low = hi_lo(w_out[t])
        wo3[t] = jnp.concatenate([hi, low], axis=0).T.astype(BF16)
        hi, low = hi_lo(w_in[t])
        w3[t] = jnp.concatenate([hi, hi, low, low], axis=0).astype(BF16)
        hi, low = hi_lo(mix[t])
        mixc[t] = jnp.concatenate([hi, low], axis=1).astype(BF16)

    arrive(send_pos)
    spots = [postab[hx, hy] for hx in range(4) for hy in range(4)]
    lanes = jnp.concatenate(spots, axis=1)
    lanes = jnp.concatenate([lanes, jnp.zeros((5, 256), F32)], axis=0)
    split = jnp.concatenate(list(three(lanes)) + [jnp.zeros((8, 256), F32)], axis=0).astype(BF16)
    for g in range(GROUPS):
        found = nn(split, signed[:, at(g)])
        found = found[0:8] + (found[8:16] + found[16:24])
        for comp in range(3):
            geo[comp, g : g + 1, :] = found[comp : comp + 1]
    ux = geo[0] / 6.0 + (step_x - 1).astype(F32)
    uy = geo[1] / 6.0 + (step_y - 1).astype(F32)
    uz = geo[2] / 6.0
    unit_sq = ux * ux + uy * uy + uz * uz
    distance = jnp.sqrt(36.0 * unit_sq + 0.01)
    inside = jnp.maximum(1.0 - unit_sq, 0.0)
    inside_live = inside * live
    geo[0] = ux
    geo[1] = uy
    geo[2] = uz
    geo[3] = ROOT3 * ux * uy
    geo[4] = ROOT3 * uy * uz
    geo[5] = uz * uz - 0.5 * (ux * ux + uy * uy)
    geo[6] = ROOT3 * ux * uz
    geo[7] = 0.5 * ROOT3 * (ux * ux - uy * uy)
    geo[8] = distance / SPACING
    geo[9] = inside * inside_live
    geo[10] = -1.0 / (SPACING * distance)
    geo[11] = (-2.0 / 36.0) * inside_live

    def row(q, g):
        return geo[q, g : g + 1, :]

    order = iota((8, 256), 0).astype(F32)

    def four_basis(x):
        hi, low = hi_lo(x)
        return jnp.concatenate([hi, low, hi, low], axis=0).astype(BF16)

    def radial(t, g):
        arg = row(8, g) - order
        envelope = row(9, g)
        pre = tn(w3[t], four_basis(jnp.exp(-(arg * arg))))
        sig = 0.5 * jnp.tanh(0.5 * pre) + 0.5
        silu = pre * sig
        hid[t, g] = silu
        dse[t, g] = sig
        units = (silu * envelope).astype(BF16)
        rad[t, g] = nn(wo3[t], jnp.concatenate([units, units], axis=0))

    def radial_grad(t, g):
        arg = row(8, g) - order
        dpre = tn(w3[t], four_basis(jnp.exp(-(arg * arg)) * arg * row(10, g)))
        sig, silu = dse[t, g], hid[t, g]
        slope = (sig + silu * (1.0 - sig)) * row(9, g)
        units = (slope * dpre + silu * row(11, g)).astype(BF16)
        change = nn(wo3[t], jnp.concatenate([units, units], axis=0))
        found = xjt[t, g]
        for part in range(3):
            lines = slice(128 * part, 128 * part + 128)
            pdf[t, g, lines, :] = (change[lines] * found).astype(BF16)

    def make_harmonics(g):
        rows = []
        for _, _, parts, first in PARTS:
            rows += [row(first + m - 1, g) * diag if first else diag for m in range(parts)]
            rows += [jnp.zeros_like(diag)]
        amat[g] = jnp.concatenate(rows, axis=0).astype(BF16)

    def groups(body, *args):
        for g in range(GROUPS):
            body(*args, g)

    groups(radial, 0)
    groups(make_harmonics)

    def gather_table(table):
        tabt[...] = table[...].reshape(256, 128).astype(F32).T.astype(BF16)

    def messages(t, g):
        found = nn(tabt[...], oh[:, at(g)])
        xjt[t, g] = found
        for part, (begin, rows, parts, first) in enumerate(PARTS):
            lines = slice(128 * part, 128 * part + 128)
            prod = (rad[t, g, lines, :] * found).astype(BF16)
            pbf[t, g, lines, :] = prod
            got = nt(amat[g, begin : begin + rows + 8, :], prod)[:rows]
            msg[t, g, 8 * first : 8 * first + rows, :] = got
            if part == 0:
                total = got
            else:
                square = got * got
                total = square[0:8]
                for m in range(1, parts):
                    total = total + square[8 * m : 8 * m + 8]
            inv[8 * g : 8 * g + 8, lines] = total

    def mixed(t):
        hi, low = hi_lo(inv[...])
        both = nn(jnp.concatenate([hi, low], axis=0).astype(BF16), mixc[t])
        return (both[64:, :128] + both[:64, 128:]) + both[:64, :128]

    def unmixed(t, cotangent):
        left = cotangent.astype(BF16)
        dinv[...] = nt(jnp.concatenate([left, left], axis=1), mixc[t])

    def message_grads(t, g, part):
        begin, rows, parts, first = PARTS[part]
        base = dinv[8 * g : 8 * g + 8, 128 * part : 128 * part + 128]
        if part == 0:
            return base
        base = base + base
        return jnp.concatenate(
            [msg[t, g, 8 * (first + m) : 8 * (first + m) + 8, :] * base for m in range(parts)],
            axis=0,
        )

    def feature_grads(t, g):
        total = None
        for part, (begin, rows, parts, first) in enumerate(PARTS):
            got = message_grads(t, g, part)
            dp = tn(
                jnp.concatenate([got, jnp.zeros((8, 128), F32)], axis=0).astype(BF16),
                amat[g, begin : begin + rows + 8, :],
            )
            term = dp * rad[t, g, 128 * part : 128 * part + 128, :]
            total = term if total is None else total + term
        dcat[:, at(g)] = total.astype(BF16)

    def scattered():
        return nt(oh[...], dcat[...])

    def separation_grads(t, g):
        plain, change = [], None
        for part, (begin, rows, parts, first) in enumerate(PARTS):
            lines = slice(128 * part, 128 * part + 128)
            left = jnp.concatenate(
                [message_grads(t, g, part), jnp.zeros((8, 128), F32)], axis=0
            ).astype(BF16)
            if part:
                both = nn(left, pbf[t, g, lines, :])
                plain += [both[8 * m : 8 * m + 8] for m in range(parts)]
            both = nn(left, pdf[t, g, lines, :])
            for m in range(parts):
                term = both[8 * m : 8 * m + 8]
                if part:
                    term = term * row(first + m - 1, g)
                change = term if change is None else change + term
        d = plain
        ax, ay, az = row(0, g), row(1, g), row(2, g)
        change = 72.0 * change
        fx = d[0] + ROOT3 * (ay * d[3] + az * d[6] + ax * d[7]) + ax * (change - d[5])
        fy = d[1] + ROOT3 * (ax * d[3] + az * d[4] - ay * d[7]) + ay * (change - d[5])
        fz = d[2] + ROOT3 * (ay * d[4] + ax * d[6]) + az * (change + 2.0 * d[5])
        whole = jnp.concatenate([fx * diag, fy * diag, fz * diag], axis=0)
        if t == 1:
            frc[:, at(g)] = whole
        else:
            frc[:, at(g)] += whole

    arrive(send_one)
    gather_table(tab1)
    groups(messages, 0)
    z_one = mixed(0)

    def own_rows(table, cx, cy):
        return table[1 + cx, 1 + cy].astype(F32)

    for cx in range(2):
        for cy in range(2):
            first = 16 * (2 * cx + cy)
            rows = z_one[first : first + 16] + own_rows(tab1, cx, cy)
            tab2[1 + cx, 1 + cy] = rows.astype(BF16)
    start(send_two)
    groups(radial, 1)
    groups(radial_grad, 0)

    arrive(send_two)
    gather_table(tab2)
    groups(messages, 1)
    z_two = mixed(1) + jnp.concatenate(
        [own_rows(tab2, cx, cy) for cx in range(2) for cy in range(2)], axis=0
    )
    sig = 0.5 * jnp.tanh(0.5 * z_two) + 0.5
    silu = z_two * sig
    out = jnp.broadcast_to(readout[...], (8, 128))
    z_grad = (sig + silu * (1.0 - sig)) * readout[...]
    unmixed(1, z_grad)
    groups(feature_grads, 1)

    def put_ghosts(target, full):
        for hx in range(4):
            for hy in range(4):
                if hx in (1, 2) and hy in (1, 2):
                    continue
                first = 16 * (4 * hx + hy)
                target[hx, hy] = full[first : first + 16].astype(target.dtype)

    full = scattered()
    put_ghosts(gs2, full)
    start(back_two)

    values = lax.dot_general(
        out, silu, (((1,), (1,)), ((), ())),
        precision=lax.Precision.HIGHEST, preferred_element_type=F32,
    )
    for cx in range(2):
        for cy in range(2):
            first = 16 * (2 * cx + cy)
            energy[cx, cy : cy + 1, :] = values[0:1, first : first + 16]

    def own_block(full):
        return jnp.concatenate(
            [full[16 * (4 * hx + hy) : 16 * (4 * hx + hy) + 16] for hx in (1, 2) for hy in (1, 2)],
            axis=0,
        )

    own_two = z_grad + own_block(full)
    groups(radial_grad, 1)
    groups(separation_grads, 1)

    def returned(target, cx, cy):
        hx, hy = 3 * cx, 3 * cy
        return (
            target[hx, 1 + cy].astype(F32)
            + target[1 + cx, hy].astype(F32)
            + target[hx, hy].astype(F32)
        )

    arrive(back_two)
    own_two = own_two + jnp.concatenate(
        [returned(gr2, cx, cy) for cx in range(2) for cy in range(2)], axis=0
    )
    unmixed(0, own_two)
    groups(feature_grads, 0)
    full = scattered()
    put_ghosts(gs1, full)
    start(back_one)
    own_one = own_two + own_block(full)
    groups(separation_grads, 0)

    hi, low = hi_lo(frc[...])
    both = nt(jnp.concatenate([hi, low], axis=0).astype(BF16), signed[...])
    both = both[:24] + both[24:]
    moved = jnp.concatenate(
        [jnp.sum(both[8 * c : 8 * c + 8], axis=0, keepdims=True) for c in range(3)], axis=0
    ) * (1.0 / 6.0)
    for hx in range(4):
        for hy in range(4):
            if hx in (1, 2) and hy in (1, 2):
                continue
            first = 16 * (4 * hx + hy)
            ps[hx, hy] = moved[:, first : first + 16]
    start(back_pos)

    arrive(back_one)
    for cx in range(2):
        for cy in range(2):
            first = 16 * (2 * cx + cy)
            fgrad[cx, cy] = own_one[first : first + 16] + returned(gr1, cx, cy)

    arrive(back_pos)
    for cx in range(2):
        for cy in range(2):
            first = 16 * (4 * (1 + cx) + 1 + cy)
            total = -(moved[:, first : first + 16] + returned(pr, cx, cy))
            for comp in range(3):
                forces[cx, comp, cy : cy + 1, :] = total[comp : comp + 1]

    for group in (send_pos, send_one, send_two, back_two, back_one, back_pos):
        for copy in group:
            copy.wait_send()


def deliver(a, b, c, a_out, b_out, c_out, sem):
    moves = [
        pltpu.make_async_copy(source, target, sem.at[k])
        for k, (source, target) in enumerate(((a, a_out), (b, b_out), (c, c_out)))
    ]
    for move in moves:
        move.start()
    for move in moves:
        move.wait()


def scratch():
    vmem = pltpu.VMEM
    return [
        vmem((2, 2, 16, 128), BF16),
        vmem((2, 3, 2, 16), F32),
        vmem((2, 2, 16), jnp.int32),
        vmem((2, 2, 16, 32), jnp.int32),
        vmem((2, 2, 16), jnp.int32),
        vmem((6, 128), F32),
        vmem((2, 8, 64), F32),
        vmem((2, 64, 384), F32),
        vmem((2, 384, 128), F32),
        vmem((1, 128), F32),
        vmem((4, 4, 16, 128), BF16),
        vmem((4, 4, 16, 128), BF16),
        vmem((4, 4, 3, 16), F32),
        vmem((4, 4, 16, 128), GRAD),
        vmem((4, 4, 16, 128), GRAD),
        vmem((4, 4, 16, 128), GRAD),
        vmem((4, 4, 16, 128), GRAD),
        vmem((4, 4, 3, 16), F32),
        vmem((4, 4, 3, 16), F32),
        vmem((256, 2048), BF16),
        vmem((256, 2048), BF16),
        vmem((8, 96, 256), BF16),
        vmem((12, 8, 256), F32),
        vmem((8, 16), F32),
        vmem((2, 8, 64, 256), F32),
        vmem((2, 8, 64, 256), F32),
        vmem((2, 8, 384, 256), F32),
        vmem((2, 8, 384, 256), BF16),
        vmem((2, 8, 384, 256), BF16),
        vmem((2, 8, 128, 256), F32),
        vmem((2, 8, 72, 128), F32),
        vmem((64, 384), F32),
        vmem((64, 384), F32),
        vmem((128, 2048), BF16),
        vmem((24, 2048), F32),
        vmem((2, 384, 128), BF16),
        vmem((2, 32, 64), BF16),
        vmem((2, 384, 256), BF16),
        vmem((128, 256), BF16),
        pltpu.SemaphoreType.DMA((10,)),
        pltpu.SemaphoreType.DMA((6, 8)),
        pltpu.SemaphoreType.DMA((6, 8)),
    ]


def shards(nx, ny, features, positions, species, neighbours, counts, gain, w_in, w_out, mix, readout):
    shape = jax.ShapeDtypeStruct
    outside = pl.BlockSpec(memory_space=pl.ANY)
    whole = pl.BlockSpec(memory_space=pltpu.VMEM)
    energy, forces, fgrad = pl.pallas_call(
        functools.partial(kernel, nx, ny),
        out_shape=(
            pltpu.VMEM((2, 2, 16), F32),
            pltpu.VMEM((2, 3, 2, 16), F32),
            pltpu.VMEM((2, 2, 16, 128), F32),
        ),
        in_specs=[outside] * 10,
        out_specs=(whole,) * 3,
        scratch_shapes=scratch(),
        compiler_params=pltpu.CompilerParams(
            collective_id=0, has_side_effects=True, vmem_limit_bytes=VLIM * 1024 * 1024
        ),
        name="potential",
    )(
        features, jnp.transpose(positions, (0, 2, 1, 3)), species, neighbours, counts, gain,
        w_in, w_out, mix, readout.reshape(1, -1),
    )
    results = (energy, forces, fgrad)
    energy, forces, fgrad = pl.pallas_call(
        deliver,
        out_shape=tuple(shape(x.shape, x.dtype) for x in results),
        in_specs=[whole] * 3,
        out_specs=(pl.BlockSpec(memory_space=pltpu.HBM),) * 3,
        scratch_shapes=[pltpu.SemaphoreType.DMA((3,))],
        compiler_params=pltpu.CompilerParams(vmem_limit_bytes=1024 * 1024),
        name="deliver",
    )(*results)
    return energy, jnp.transpose(forces, (0, 2, 1, 3)), fgrad


def solution(mesh):
    placed = (
        P("gx", "gy", None, None), P("gx", "gy", None, None), P("gx", "gy", None),
        P("gx", "gy", None, None), P("gx", "gy", None), P(), P(), P(), P(), P(),
    )
    return jax.shard_map(
        functools.partial(shards, mesh.shape["gx"], mesh.shape["gy"]),
        mesh=mesh,
        in_specs=placed,
        out_specs=(P("gx", "gy", None), P("gx", "gy", None, None), P("gx", "gy", None, None)),
        check_vma=False,
    )
```

```python
import functools

import jax
import jax.numpy as jnp
from jax import lax
from jax.experimental import pallas as pl
from jax.experimental.pallas import tpu as pltpu
from jax.sharding import PartitionSpec as P

F32 = jnp.float32
BF16 = jnp.bfloat16
MESH = pl.DeviceIdType.MESH
GRAD = BF16
DIRS = tuple((dx, dy) for dx in (-1, 0, 1) for dy in (-1, 0, 1) if (dx, dy) != (0, 0))
VLIM = 60
SPACING = 6.0 / 7.0
ROOT3 = 3.0**0.5
GROUPS = 8
PARTS = ((0, 8, 1, 0), (16, 24, 3, 1), (48, 40, 5, 4))


def nn(a, b):
    return lax.dot_general(a, b, (((1,), (0,)), ((), ())), preferred_element_type=F32)


def nt(a, b):
    return lax.dot_general(a, b, (((1,), (1,)), ((), ())), preferred_element_type=F32)


def tn(a, b):
    return lax.dot_general(a, b, (((0,), (0,)), ((), ())), preferred_element_type=F32)


def hi_lo(x):
    hi = x.astype(BF16).astype(F32)
    return hi, x - hi


def three(x):
    hi, rest = hi_lo(x)
    mid, low = hi_lo(rest)
    return hi, mid, low


def iota(shape, dim):
    return lax.broadcasted_iota(jnp.int32, shape, dim)


def kernel(
    nx, ny,
    feat_h, pos_h, spec_h, nb_h, cnt_h, gain_h, w_in_h, w_out_h, mix_h, readout_h,
    energy, forces, fgrad,
    feat, pos, spec, nb, cnt, gain, w_in, w_out, mix, readout,
    tab1, tab2, postab, gs2, gr2, gs1, gr1, ps, pr,
    oh, signed, amat, geo, atom, hid, dse, rad, pbf, pdf, xjt, msg, inv, dinv, dcat, frc,
    wo3, w3, mixc, tabt, units,
    lsem, ssem, rsem,
):
    gx, gy = lax.axis_index("gx"), lax.axis_index("gy")
    peers = [(lax.rem(gx + (dx + nx), nx), lax.rem(gy + (dy + ny), ny)) for dx, dy in DIRS]

    barrier = pltpu.get_barrier_semaphore()
    for peer in peers:
        pl.semaphore_signal(barrier, inc=1, device_id=peer, device_id_type=MESH)

    def pick(d, up, down, mid):
        return up if d == 1 else down if d == -1 else mid

    def copies(slot, src, dst, src_at, dst_at):
        out = []
        for k, (dx, dy) in enumerate(DIRS):
            out.append(
                pltpu.make_async_remote_copy(
                    src_ref=src.at[src_at(dx), src_at(dy)],
                    dst_ref=dst.at[dst_at(dx), dst_at(dy)],
                    send_sem=ssem.at[slot, k],
                    recv_sem=rsem.at[slot, k],
                    device_id=peers[k],
                    device_id_type=MESH,
                )
            )
        return out

    centre = pl.ds(1, 2)

    def owned_at(d):
        return pick(d, 2, 1, centre)

    def halo_at(d):
        return pick(d, 0, 3, centre)

    def ghost_at(d):
        return pick(d, 3, 0, centre)

    send_pos = copies(0, postab, postab, owned_at, halo_at)
    send_one = copies(1, tab1, tab1, owned_at, halo_at)
    send_two = copies(2, tab2, tab2, owned_at, halo_at)
    back_two = copies(3, gs2, gr2, ghost_at, halo_at)
    back_one = copies(4, gs1, gr1, ghost_at, halo_at)
    back_pos = copies(5, ps, pr, ghost_at, halo_at)

    def start(group):
        for copy in group:
            copy.start()

    def arrive(group):
        for copy in group:
            copy.wait_recv()

    sources = (pos_h, spec_h, feat_h, gain_h, nb_h, cnt_h, w_in_h, w_out_h, mix_h, readout_h)
    targets = (pos, spec, feat, gain, nb, cnt, w_in, w_out, mix, readout)
    loads = [
        pltpu.make_async_copy(source, target, lsem.at[k])
        for k, (source, target) in enumerate(zip(sources, targets))
    ]
    start(loads)

    loads[0].wait()
    for cx in range(2):
        for cy in range(2):
            for comp in range(3):
                postab[1 + cx, 1 + cy, comp : comp + 1, :] = pos[cx, comp, cy : cy + 1, :]
    for k in (1, 2, 3):
        loads[k].wait()
    kinds = gain.shape[0]
    for cx in range(2):
        for cy in range(2):
            onehot = (iota((kinds, 16), 0) == spec[cx, cy : cy + 1, :]).astype(F32)
            rows = lax.dot_general(
                onehot, gain[...], (((0,), (0,)), ((), ())),
                precision=lax.Precision.HIGHEST, preferred_element_type=F32,
            )
            tab1[1 + cx, 1 + cy] = (feat[cx, cy].astype(F32) * rows).astype(BF16)

    pl.semaphore_wait(barrier, len(DIRS))
    start(send_pos)
    start(send_one)

    for k in (4, 5):
        loads[k].wait()
    sub = iota((8, 256), 0)
    lane = iota((8, 256), 1)
    lane_atom = lax.shift_right_logical(lane, 5)
    diag = (sub == lane_atom).astype(F32)
    codes = nb[...].reshape(64, 32).astype(F32).astype(BF16)
    tile = (iota((32, 256), 0) == (iota((32, 256), 1) & 31)).astype(BF16)
    repeated = nn(codes, tile)
    keep = (iota((64, 256), 0) & 7) == lax.shift_right_logical(iota((64, 256), 1), 5)
    repeated = jnp.where(keep, repeated, 0.0).astype(BF16)
    gather8 = (iota((8, 64), 0) == lax.shift_right_logical(iota((8, 64), 1), 3)).astype(BF16)
    code = nn(gather8, repeated).astype(jnp.int32)
    offset = lax.shift_right_logical(code, 4)
    step_x = (offset >= 3).astype(jnp.int32) + (offset >= 6).astype(jnp.int32)
    step_y = offset - 3 * step_x
    halo_x = lax.shift_right_logical(sub, 2) + step_x
    halo_y = (lax.shift_right_logical(sub, 1) & 1) + step_y
    index = (halo_x * 4 + halo_y) * 16 + (code & 15)

    for g in range(GROUPS):
        atom[g : g + 1, :] = cnt[g // 4, g // 2 % 2 : g // 2 % 2 + 1, :].astype(F32)
    half16 = lax.shift_right_logical(iota((8, 16), 1), 3) == (iota((8, 16), 0) & 1)
    spread = (
        (iota((16, 256), 0) & 7) == lax.shift_right_logical(iota((16, 256), 1), 5)
    ).astype(BF16)
    count = nn(jnp.where(half16, atom[...], 0.0).astype(BF16), spread)
    live = ((lane & 31).astype(F32) < count).astype(F32)

    def at(g):
        return slice(256 * g, 256 * g + 256)

    candidate = iota((256, 256), 0)
    for g in range(GROUPS):
        found = (candidate == index[g : g + 1]).astype(F32)
        oh[:, at(g)] = found.astype(BF16)
        mine = 16 * (4 * (1 + g // 4) + 1 + g // 2 % 2) + 8 * (g % 2)
        signed[:, at(g)] = jnp.concatenate(
            [found[:mine], found[mine : mine + 8] - diag, found[mine + 8 :]], axis=0
        ).astype(BF16)

    for k in (6, 7, 8, 9):
        loads[k].wait()
    for t in range(2):
        hi, low = hi_lo(w_out[t])
        wo3[t] = jnp.concatenate([hi, low], axis=0).T.astype(BF16)
        hi, low = hi_lo(w_in[t])
        w3[t] = jnp.concatenate([hi, hi, low, low], axis=0).astype(BF16)
        hi, low = hi_lo(mix[t])
        mixc[t] = jnp.concatenate([hi, low], axis=1).astype(BF16)

    arrive(send_pos)
    spots = [postab[hx, hy] for hx in range(4) for hy in range(4)]
    lanes = jnp.concatenate(spots, axis=1)
    lanes = jnp.concatenate([lanes, jnp.zeros((5, 256), F32)], axis=0)
    split = jnp.concatenate(list(three(lanes)) + [jnp.zeros((8, 256), F32)], axis=0).astype(BF16)
    for g in range(GROUPS):
        found = nn(split, signed[:, at(g)])
        found = found[0:8] + (found[8:16] + found[16:24])
        for comp in range(3):
            geo[comp, g : g + 1, :] = found[comp : comp + 1]
    ux = geo[0] / 6.0 + (step_x - 1).astype(F32)
    uy = geo[1] / 6.0 + (step_y - 1).astype(F32)
    uz = geo[2] / 6.0
    unit_sq = ux * ux + uy * uy + uz * uz
    distance = jnp.sqrt(36.0 * unit_sq + 0.01)
    inside = jnp.maximum(1.0 - unit_sq, 0.0)
    inside_live = inside * live
    geo[0] = ux
    geo[1] = uy
    geo[2] = uz
    geo[3] = ROOT3 * ux * uy
    geo[4] = ROOT3 * uy * uz
    geo[5] = uz * uz - 0.5 * (ux * ux + uy * uy)
    geo[6] = ROOT3 * ux * uz
    geo[7] = 0.5 * ROOT3 * (ux * ux - uy * uy)
    geo[8] = distance / SPACING
    geo[9] = inside * inside_live
    geo[10] = -1.0 / (SPACING * distance)
    geo[11] = (-2.0 / 36.0) * inside_live

    def row(q, g):
        return geo[q, g : g + 1, :]

    order = iota((8, 256), 0).astype(F32)

    def four_basis(x):
        hi, low = hi_lo(x)
        return jnp.concatenate([hi, low, hi, low], axis=0).astype(BF16)

    def radial(t):
        groups(hidden_units, t)
        rad[t] = nn(wo3[t], units[...])

    def hidden_units(t, g):
        arg = row(8, g) - order
        envelope = row(9, g)
        pre = tn(w3[t], four_basis(jnp.exp(-(arg * arg))))
        sig = 0.5 * jnp.tanh(0.5 * pre) + 0.5
        silu = pre * sig
        hid[t, g] = silu
        dse[t, g] = sig
        half = (silu * envelope).astype(BF16)
        units[:, at(g)] = jnp.concatenate([half, half], axis=0)

    def radial_grad(t, g):
        arg = row(8, g) - order
        dpre = tn(w3[t], four_basis(jnp.exp(-(arg * arg)) * arg * row(10, g)))
        sig, silu = dse[t, g], hid[t, g]
        slope = (sig + silu * (1.0 - sig)) * row(9, g)
        half = (slope * dpre + silu * row(11, g)).astype(BF16)
        units[:, at(g)] = jnp.concatenate([half, half], axis=0)

    def radial_change(t, g):
        change = nn(wo3[t], units[:, at(g)])
        found = xjt[t, :, at(g)]
        for part in range(3):
            lines = slice(128 * part, 128 * part + 128)
            pdf[t, g, lines, :] = (change[lines] * found).astype(BF16)

    def make_harmonics(g):
        rows = []
        for _, _, parts, first in PARTS:
            rows += [row(first + m - 1, g) * diag if first else diag for m in range(parts)]
            rows += [jnp.zeros_like(diag)]
        amat[g] = jnp.concatenate(rows, axis=0).astype(BF16)

    def groups(body, *args):
        for g in range(GROUPS):
            body(*args, g)

    radial(0)
    groups(make_harmonics)

    def gather_table(table):
        tabt[...] = table[...].reshape(256, 128).astype(F32).T.astype(BF16)

    def messages(t):
        xjt[t] = nn(tabt[...], oh[...])
        groups(products, t)
        groups(message_sums, t)

    def products(t, g):
        found = xjt[t, :, at(g)]
        for part in range(3):
            lines = slice(128 * part, 128 * part + 128)
            pbf[t, g, lines, :] = (rad[t, lines, at(g)] * found).astype(BF16)

    def message_sums(t, g):
        for part, (begin, rows, parts, first) in enumerate(PARTS):
            lines = slice(128 * part, 128 * part + 128)
            got = nt(amat[g, begin : begin + rows + 8, :], pbf[t, g, lines, :])[:rows]
            msg[t, g, 8 * first : 8 * first + rows, :] = got
            if part == 0:
                total = got
            else:
                square = got * got
                total = square[0:8]
                for m in range(1, parts):
                    total = total + square[8 * m : 8 * m + 8]
            inv[8 * g : 8 * g + 8, lines] = total

    def mixed(t):
        hi, low = hi_lo(inv[...])
        both = nn(jnp.concatenate([hi, low], axis=0).astype(BF16), mixc[t])
        return (both[64:, :128] + both[:64, 128:]) + both[:64, :128]

    def unmixed(t, cotangent):
        left = cotangent.astype(BF16)
        dinv[...] = nt(jnp.concatenate([left, left], axis=1), mixc[t])

    def message_grads(t, g, part):
        begin, rows, parts, first = PARTS[part]
        base = dinv[8 * g : 8 * g + 8, 128 * part : 128 * part + 128]
        if part == 0:
            return base
        base = base + base
        return jnp.concatenate(
            [msg[t, g, 8 * (first + m) : 8 * (first + m) + 8, :] * base for m in range(parts)],
            axis=0,
        )

    def feature_grads(t, g):
        total = None
        for part, (begin, rows, parts, first) in enumerate(PARTS):
            got = message_grads(t, g, part)
            dp = tn(
                jnp.concatenate([got, jnp.zeros((8, 128), F32)], axis=0).astype(BF16),
                amat[g, begin : begin + rows + 8, :],
            )
            term = dp * rad[t, 128 * part : 128 * part + 128, at(g)]
            total = term if total is None else total + term
        dcat[:, at(g)] = total.astype(BF16)

    def scattered():
        return nt(oh[...], dcat[...])

    def separation_grads(t, g):
        plain, change = [], None
        for part, (begin, rows, parts, first) in enumerate(PARTS):
            lines = slice(128 * part, 128 * part + 128)
            left = jnp.concatenate(
                [message_grads(t, g, part), jnp.zeros((8, 128), F32)], axis=0
            ).astype(BF16)
            if part:
                both = nn(left, pbf[t, g, lines, :])
                plain += [both[8 * m : 8 * m + 8] for m in range(parts)]
            both = nn(left, pdf[t, g, lines, :])
            for m in range(parts):
                term = both[8 * m : 8 * m + 8]
                if part:
                    term = term * row(first + m - 1, g)
                change = term if change is None else change + term
        d = plain
        ax, ay, az = row(0, g), row(1, g), row(2, g)
        change = 72.0 * change
        fx = d[0] + ROOT3 * (ay * d[3] + az * d[6] + ax * d[7]) + ax * (change - d[5])
        fy = d[1] + ROOT3 * (ax * d[3] + az * d[4] - ay * d[7]) + ay * (change - d[5])
        fz = d[2] + ROOT3 * (ay * d[4] + ax * d[6]) + az * (change + 2.0 * d[5])
        whole = jnp.concatenate([fx * diag, fy * diag, fz * diag], axis=0)
        if t == 1:
            frc[:, at(g)] = whole
        else:
            frc[:, at(g)] += whole

    arrive(send_one)
    gather_table(tab1)
    messages(0)
    z_one = mixed(0)

    def own_rows(table, cx, cy):
        return table[1 + cx, 1 + cy].astype(F32)

    for cx in range(2):
        for cy in range(2):
            first = 16 * (2 * cx + cy)
            rows = z_one[first : first + 16] + own_rows(tab1, cx, cy)
            tab2[1 + cx, 1 + cy] = rows.astype(BF16)
    start(send_two)
    radial(1)
    groups(radial_grad, 0)
    groups(radial_change, 0)

    arrive(send_two)
    gather_table(tab2)
    messages(1)
    z_two = mixed(1) + jnp.concatenate(
        [own_rows(tab2, cx, cy) for cx in range(2) for cy in range(2)], axis=0
    )
    sig = 0.5 * jnp.tanh(0.5 * z_two) + 0.5
    silu = z_two * sig
    out = jnp.broadcast_to(readout[...], (8, 128))
    z_grad = (sig + silu * (1.0 - sig)) * readout[...]
    unmixed(1, z_grad)
    groups(feature_grads, 1)

    def put_ghosts(target, full):
        for hx in range(4):
            for hy in range(4):
                if hx in (1, 2) and hy in (1, 2):
                    continue
                first = 16 * (4 * hx + hy)
                target[hx, hy] = full[first : first + 16].astype(target.dtype)

    full = scattered()
    put_ghosts(gs2, full)
    start(back_two)

    values = lax.dot_general(
        out, silu, (((1,), (1,)), ((), ())),
        precision=lax.Precision.HIGHEST, preferred_element_type=F32,
    )
    for cx in range(2):
        for cy in range(2):
            first = 16 * (2 * cx + cy)
            energy[cx, cy : cy + 1, :] = values[0:1, first : first + 16]

    def own_block(full):
        return jnp.concatenate(
            [full[16 * (4 * hx + hy) : 16 * (4 * hx + hy) + 16] for hx in (1, 2) for hy in (1, 2)],
            axis=0,
        )

    own_two = z_grad + own_block(full)
    groups(radial_grad, 1)
    groups(radial_change, 1)
    groups(separation_grads, 1)

    def returned(target, cx, cy):
        hx, hy = 3 * cx, 3 * cy
        return (
            target[hx, 1 + cy].astype(F32)
            + target[1 + cx, hy].astype(F32)
            + target[hx, hy].astype(F32)
        )

    arrive(back_two)
    own_two = own_two + jnp.concatenate(
        [returned(gr2, cx, cy) for cx in range(2) for cy in range(2)], axis=0
    )
    unmixed(0, own_two)
    groups(feature_grads, 0)
    full = scattered()
    put_ghosts(gs1, full)
    start(back_one)
    own_one = own_two + own_block(full)
    groups(separation_grads, 0)

    hi, low = hi_lo(frc[...])
    both = nt(jnp.concatenate([hi, low], axis=0).astype(BF16), signed[...])
    both = both[:24] + both[24:]
    moved = jnp.concatenate(
        [jnp.sum(both[8 * c : 8 * c + 8], axis=0, keepdims=True) for c in range(3)], axis=0
    ) * (1.0 / 6.0)
    for hx in range(4):
        for hy in range(4):
            if hx in (1, 2) and hy in (1, 2):
                continue
            first = 16 * (4 * hx + hy)
            ps[hx, hy] = moved[:, first : first + 16]
    start(back_pos)

    arrive(back_one)
    for cx in range(2):
        for cy in range(2):
            first = 16 * (2 * cx + cy)
            fgrad[cx, cy] = own_one[first : first + 16] + returned(gr1, cx, cy)

    arrive(back_pos)
    for cx in range(2):
        for cy in range(2):
            first = 16 * (4 * (1 + cx) + 1 + cy)
            total = -(moved[:, first : first + 16] + returned(pr, cx, cy))
            for comp in range(3):
                forces[cx, comp, cy : cy + 1, :] = total[comp : comp + 1]

    for group in (send_pos, send_one, send_two, back_two, back_one, back_pos):
        for copy in group:
            copy.wait_send()


def deliver(a, b, c, a_out, b_out, c_out, sem):
    moves = [
        pltpu.make_async_copy(source, target, sem.at[k])
        for k, (source, target) in enumerate(((a, a_out), (b, b_out), (c, c_out)))
    ]
    for move in moves:
        move.start()
    for move in moves:
        move.wait()


def scratch():
    vmem = pltpu.VMEM
    return [
        vmem((2, 2, 16, 128), BF16),
        vmem((2, 3, 2, 16), F32),
        vmem((2, 2, 16), jnp.int32),
        vmem((2, 2, 16, 32), jnp.int32),
        vmem((2, 2, 16), jnp.int32),
        vmem((6, 128), F32),
        vmem((2, 8, 64), F32),
        vmem((2, 64, 384), F32),
        vmem((2, 384, 128), F32),
        vmem((1, 128), F32),
        vmem((4, 4, 16, 128), BF16),
        vmem((4, 4, 16, 128), BF16),
        vmem((4, 4, 3, 16), F32),
        vmem((4, 4, 16, 128), GRAD),
        vmem((4, 4, 16, 128), GRAD),
        vmem((4, 4, 16, 128), GRAD),
        vmem((4, 4, 16, 128), GRAD),
        vmem((4, 4, 3, 16), F32),
        vmem((4, 4, 3, 16), F32),
        vmem((256, 2048), BF16),
        vmem((256, 2048), BF16),
        vmem((8, 96, 256), BF16),
        vmem((12, 8, 256), F32),
        vmem((8, 16), F32),
        vmem((2, 8, 64, 256), F32),
        vmem((2, 8, 64, 256), F32),
        vmem((2, 384, 2048), F32),
        vmem((2, 8, 384, 256), BF16),
        vmem((2, 8, 384, 256), BF16),
        vmem((2, 128, 2048), F32),
        vmem((2, 8, 72, 128), F32),
        vmem((64, 384), F32),
        vmem((64, 384), F32),
        vmem((128, 2048), BF16),
        vmem((24, 2048), F32),
        vmem((2, 384, 128), BF16),
        vmem((2, 32, 64), BF16),
        vmem((2, 384, 256), BF16),
        vmem((128, 256), BF16),
        vmem((128, 2048), BF16),
        pltpu.SemaphoreType.DMA((10,)),
        pltpu.SemaphoreType.DMA((6, 8)),
        pltpu.SemaphoreType.DMA((6, 8)),
    ]


def shards(nx, ny, features, positions, species, neighbours, counts, gain, w_in, w_out, mix, readout):
    shape = jax.ShapeDtypeStruct
    outside = pl.BlockSpec(memory_space=pl.ANY)
    whole = pl.BlockSpec(memory_space=pltpu.VMEM)
    energy, forces, fgrad = pl.pallas_call(
        functools.partial(kernel, nx, ny),
        out_shape=(
            pltpu.VMEM((2, 2, 16), F32),
            pltpu.VMEM((2, 3, 2, 16), F32),
            pltpu.VMEM((2, 2, 16, 128), F32),
        ),
        in_specs=[outside] * 10,
        out_specs=(whole,) * 3,
        scratch_shapes=scratch(),
        compiler_params=pltpu.CompilerParams(
            collective_id=0, has_side_effects=True, vmem_limit_bytes=VLIM * 1024 * 1024
        ),
        name="potential",
    )(
        features, jnp.transpose(positions, (0, 2, 1, 3)), species, neighbours, counts, gain,
        w_in, w_out, mix, readout.reshape(1, -1),
    )
    results = (energy, forces, fgrad)
    energy, forces, fgrad = pl.pallas_call(
        deliver,
        out_shape=tuple(shape(x.shape, x.dtype) for x in results),
        in_specs=[whole] * 3,
        out_specs=(pl.BlockSpec(memory_space=pltpu.HBM),) * 3,
        scratch_shapes=[pltpu.SemaphoreType.DMA((3,))],
        compiler_params=pltpu.CompilerParams(vmem_limit_bytes=1024 * 1024),
        name="deliver",
    )(*results)
    return energy, jnp.transpose(forces, (0, 2, 1, 3)), fgrad


def solution(mesh):
    placed = (
        P("gx", "gy", None, None), P("gx", "gy", None, None), P("gx", "gy", None),
        P("gx", "gy", None, None), P("gx", "gy", None), P(), P(), P(), P(), P(),
    )
    return jax.shard_map(
        functools.partial(shards, mesh.shape["gx"], mesh.shape["gy"]),
        mesh=mesh,
        in_specs=placed,
        out_specs=(P("gx", "gy", None), P("gx", "gy", None, None), P("gx", "gy", None, None)),
        check_vma=False,
    )
```

```python
import functools

import jax
import jax.numpy as jnp
from jax import lax
from jax.experimental import pallas as pl
from jax.experimental.pallas import tpu as pltpu
from jax.sharding import PartitionSpec as P

F32 = jnp.float32
BF16 = jnp.bfloat16
MESH = pl.DeviceIdType.MESH
GRAD = BF16
DIRS = ((1, 1), (1, -1), (-1, 1), (-1, -1), (1, 0), (-1, 0), (0, 1), (0, -1))
VLIM = 60
SPACING = 6.0 / 7.0
ROOT3 = 3.0**0.5
GROUPS = 8
PARTS = ((0, 8, 1, 0), (16, 24, 3, 1), (48, 40, 5, 4))


def nn(a, b):
    return lax.dot_general(a, b, (((1,), (0,)), ((), ())), preferred_element_type=F32)


def nt(a, b):
    return lax.dot_general(a, b, (((1,), (1,)), ((), ())), preferred_element_type=F32)


def tn(a, b):
    return lax.dot_general(a, b, (((0,), (0,)), ((), ())), preferred_element_type=F32)


def hi_lo(x):
    hi = x.astype(BF16).astype(F32)
    return hi, x - hi


def three(x):
    hi, rest = hi_lo(x)
    mid, low = hi_lo(rest)
    return hi, mid, low


def iota(shape, dim):
    return lax.broadcasted_iota(jnp.int32, shape, dim)


def kernel(
    nx, ny,
    feat_h, pos_h, spec_h, nb_h, cnt_h, gain_h, w_in_h, w_out_h, mix_h, readout_h,
    energy, forces, fgrad,
    feat, pos, spec, nb, cnt, gain, w_in, w_out, mix, readout,
    tab1, tab2, placed, postab, gs2, gr2, gs1, gr1, ps, pr,
    oh, signed, amat, geo, atom, hid, dse, rad, pbf, pdf, xjt, msg, inv, dinv, dcat, frc,
    wo3, w3, mixc, tabt, units, basis, pre, dmsg,
    lsem, ssem, rsem,
):
    gx, gy = lax.axis_index("gx"), lax.axis_index("gy")
    rows = {0: gx, 1: lax.rem(gx + 1, nx), -1: lax.rem(gx + (nx - 1), nx)}
    cols = {0: gy, 1: lax.rem(gy + 1, ny), -1: lax.rem(gy + (ny - 1), ny)}
    peers = [(rows[dx], cols[dy]) for dx, dy in DIRS]

    barrier = pltpu.get_barrier_semaphore()
    for peer in peers:
        pl.semaphore_signal(barrier, inc=1, device_id=peer, device_id_type=MESH)

    def pick(d, up, down, mid):
        return up if d == 1 else down if d == -1 else mid

    def copies(slot, src, dst, src_at, dst_at):
        out = []
        for k, (dx, dy) in enumerate(DIRS):
            out.append(
                pltpu.make_async_remote_copy(
                    src_ref=src.at[src_at(dx), src_at(dy)],
                    dst_ref=dst.at[dst_at(dx), dst_at(dy)],
                    send_sem=ssem.at[slot, k],
                    recv_sem=rsem.at[slot, k],
                    device_id=peers[k],
                    device_id_type=MESH,
                )
            )
        return out

    centre = pl.ds(1, 2)

    def owned_at(d):
        return pick(d, 2, 1, centre)

    def halo_at(d):
        return pick(d, 0, 3, centre)

    def ghost_at(d):
        return pick(d, 3, 0, centre)

    send_pos = copies(0, placed, postab, halo_at, halo_at)
    send_one = copies(1, tab1, tab1, owned_at, halo_at)
    send_two = copies(2, tab2, tab2, owned_at, halo_at)
    back_two = copies(3, gs2, gr2, ghost_at, halo_at)
    back_one = copies(4, gs1, gr1, ghost_at, halo_at)
    back_pos = copies(5, ps, pr, ghost_at, halo_at)

    def start(group):
        for copy in group:
            copy.start()

    def arrive(group):
        for copy in group:
            copy.wait_recv()

    def sent(group):
        for copy in group:
            copy.wait_send()

    sources = (pos_h, spec_h, feat_h, gain_h, nb_h, cnt_h, w_in_h, w_out_h, mix_h, readout_h)
    targets = (pos, spec, feat, gain, nb, cnt, w_in, w_out, mix, readout)
    loads = [
        pltpu.make_async_copy(source, target, lsem.at[k])
        for k, (source, target) in enumerate(zip(sources, targets))
    ]
    start(loads)

    loads[0].wait()
    for hx in range(4):
        for hy in range(4):
            cx, cy = (1, 0, 1, 0)[hx], (1, 0, 1, 0)[hy]
            column = jnp.concatenate([pos[cx, c, cy : cy + 1, :] for c in range(3)], axis=0)
            before = 16 * (4 * (hx % 2) + hy)
            parts = [jnp.zeros((3, before), F32)] if before else []
            parts += [column]
            parts += [jnp.zeros((3, 112 - before), F32)] if before < 112 else []
            placed[hx, hy] = jnp.concatenate(parts, axis=1)
    for k in (1, 2, 3):
        loads[k].wait()
    kinds = gain.shape[0]
    for cx in range(2):
        for cy in range(2):
            onehot = (iota((kinds, 16), 0) == spec[cx, cy : cy + 1, :]).astype(F32)
            rows = lax.dot_general(
                onehot, gain[...], (((0,), (0,)), ((), ())),
                precision=lax.Precision.HIGHEST, preferred_element_type=F32,
            )
            tab1[1 + cx, 1 + cy] = (feat[cx, cy].astype(F32) * rows).astype(BF16)

    pl.semaphore_wait(barrier, len(DIRS))
    start(send_pos)
    start(send_one)

    for k in (4, 5):
        loads[k].wait()
    sub = iota((8, 256), 0)
    lane = iota((8, 256), 1)
    lane_atom = lax.shift_right_logical(lane, 5)
    diag = (sub == lane_atom).astype(F32)
    codes = nb[...].reshape(64, 32).astype(F32).astype(BF16)
    tile = (iota((32, 256), 0) == (iota((32, 256), 1) & 31)).astype(BF16)
    repeated = nn(codes, tile)
    keep = (iota((64, 256), 0) & 7) == lax.shift_right_logical(iota((64, 256), 1), 5)
    repeated = jnp.where(keep, repeated, 0.0).astype(BF16)
    gather8 = (iota((8, 64), 0) == lax.shift_right_logical(iota((8, 64), 1), 3)).astype(BF16)
    code = nn(gather8, repeated).astype(jnp.int32)
    offset = lax.shift_right_logical(code, 4)
    step_x = (offset >= 3).astype(jnp.int32) + (offset >= 6).astype(jnp.int32)
    step_y = offset - 3 * step_x
    halo_x = lax.shift_right_logical(sub, 2) + step_x
    halo_y = (lax.shift_right_logical(sub, 1) & 1) + step_y
    index = (halo_x * 4 + halo_y) * 16 + (code & 15)

    for g in range(GROUPS):
        atom[g : g + 1, :] = cnt[g // 4, g // 2 % 2 : g // 2 % 2 + 1, :].astype(F32)
    half16 = lax.shift_right_logical(iota((8, 16), 1), 3) == (iota((8, 16), 0) & 1)
    spread = (
        (iota((16, 256), 0) & 7) == lax.shift_right_logical(iota((16, 256), 1), 5)
    ).astype(BF16)
    count = nn(jnp.where(half16, atom[...], 0.0).astype(BF16), spread)
    live = ((lane & 31).astype(F32) < count).astype(F32)

    def at(g):
        return slice(256 * g, 256 * g + 256)

    candidate = iota((256, 256), 0)
    for g in range(GROUPS):
        found = (candidate == index[g : g + 1]).astype(F32)
        oh[:, at(g)] = found.astype(BF16)
        mine = 16 * (4 * (1 + g // 4) + 1 + g // 2 % 2) + 8 * (g % 2)
        signed[:, at(g)] = jnp.concatenate(
            [found[:mine], found[mine : mine + 8] - diag, found[mine + 8 :]], axis=0
        ).astype(BF16)

    for k in (6, 7, 8, 9):
        loads[k].wait()
    for t in range(2):
        hi, low = hi_lo(w_out[t])
        wo3[t] = jnp.concatenate([hi, low], axis=0).T.astype(BF16)
        hi, low = hi_lo(w_in[t])
        w3[t] = jnp.concatenate([hi, hi, low, low], axis=0).astype(BF16)
        hi, low = hi_lo(mix[t])
        mixc[t] = jnp.concatenate([hi, low], axis=1).astype(BF16)

    arrive(send_pos)
    def spot(hx, hy):
        return placed[hx, hy] if hx in (1, 2) and hy in (1, 2) else postab[hx, hy]

    sides = []
    for side in range(2):
        eight = [spot(2 * side + k // 4, k % 4) for k in range(8)]
        while len(eight) > 1:
            eight = [a + b for a, b in zip(eight[::2], eight[1::2])]
        sides += eight
    lanes = jnp.concatenate(sides, axis=1)
    lanes = jnp.concatenate([lanes, jnp.zeros((5, 256), F32)], axis=0)
    split = jnp.concatenate(list(three(lanes)) + [jnp.zeros((8, 256), F32)], axis=0).astype(BF16)
    for g in range(GROUPS):
        found = nn(split, signed[:, at(g)])
        found = found[0:8] + (found[8:16] + found[16:24])
        for comp in range(3):
            geo[comp, g : g + 1, :] = found[comp : comp + 1]
    ux = geo[0] / 6.0 + (step_x - 1).astype(F32)
    uy = geo[1] / 6.0 + (step_y - 1).astype(F32)
    uz = geo[2] / 6.0
    unit_sq = ux * ux + uy * uy + uz * uz
    distance = jnp.sqrt(36.0 * unit_sq + 0.01)
    inside = jnp.maximum(1.0 - unit_sq, 0.0)
    inside_live = inside * live
    geo[0] = ux
    geo[1] = uy
    geo[2] = uz
    geo[3] = ROOT3 * ux * uy
    geo[4] = ROOT3 * uy * uz
    geo[5] = uz * uz - 0.5 * (ux * ux + uy * uy)
    geo[6] = ROOT3 * ux * uz
    geo[7] = 0.5 * ROOT3 * (ux * ux - uy * uy)
    geo[8] = distance / SPACING
    geo[9] = inside * inside_live
    geo[10] = -1.0 / (SPACING * distance)
    geo[11] = (-2.0 / 36.0) * inside_live

    def row(q, g):
        return geo[q, g : g + 1, :]

    order = iota((8, 256), 0).astype(F32)

    def four_basis(x):
        hi, low = hi_lo(x)
        return jnp.concatenate([hi, low, hi, low], axis=0).astype(BF16)

    def basis_rows(g):
        arg = row(8, g) - order
        basis[:, at(g)] = four_basis(jnp.exp(-(arg * arg)))

    def slope_rows(g):
        arg = row(8, g) - order
        basis[:, at(g)] = four_basis(jnp.exp(-(arg * arg)) * arg * row(10, g))

    def radial(t):
        pre[...] = tn(w3[t], basis[...])
        groups(hidden_units, t)
        rad[t] = nn(wo3[t], units[...])

    def hidden_units(t, g):
        envelope = row(9, g)
        value = pre[:, at(g)]
        sig = 0.5 * jnp.tanh(0.5 * value) + 0.5
        silu = value * sig
        hid[t, g] = silu
        dse[t, g] = sig
        half = (silu * envelope).astype(BF16)
        units[:, at(g)] = jnp.concatenate([half, half], axis=0)

    def radial_grad(t):
        pre[...] = tn(w3[t], basis[...])
        groups(unit_slopes, t)
        groups(radial_change, t)

    def unit_slopes(t, g):
        dpre = pre[:, at(g)]
        sig, silu = dse[t, g], hid[t, g]
        slope = (sig + silu * (1.0 - sig)) * row(9, g)
        half = (slope * dpre + silu * row(11, g)).astype(BF16)
        units[:, at(g)] = jnp.concatenate([half, half], axis=0)

    def radial_change(t, g):
        change = nn(wo3[t], units[:, at(g)])
        found = xjt[t, :, at(g)]
        for part in range(3):
            lines = slice(128 * part, 128 * part + 128)
            pdf[t, g, lines, :] = (change[lines] * found).astype(BF16)

    def make_harmonics(g):
        rows = []
        for _, _, parts, first in PARTS:
            rows += [row(first + m - 1, g) * diag if first else diag for m in range(parts)]
            rows += [jnp.zeros_like(diag)]
        amat[g] = jnp.concatenate(rows, axis=0).astype(BF16)

    def groups(body, *args):
        for g in range(GROUPS):
            body(*args, g)

    groups(basis_rows)
    radial(0)
    groups(make_harmonics)

    def gather_table(table):
        tabt[...] = table[...].reshape(256, 128).astype(F32).T.astype(BF16)

    def messages(t):
        xjt[t] = nn(tabt[...], oh[...])
        groups(products, t)
        groups(message_sums, t)

    def products(t, g):
        found = xjt[t, :, at(g)]
        for part in range(3):
            lines = slice(128 * part, 128 * part + 128)
            pbf[t, g, lines, :] = (rad[t, lines, at(g)] * found).astype(BF16)

    def message_sums(t, g):
        for part, (begin, rows, parts, first) in enumerate(PARTS):
            lines = slice(128 * part, 128 * part + 128)
            got = nt(amat[g, begin : begin + rows + 8, :], pbf[t, g, lines, :])[:rows]
            msg[t, g, 8 * first : 8 * first + rows, :] = got
            if part == 0:
                total = got
            else:
                square = got * got
                total = square[0:8]
                for m in range(1, parts):
                    total = total + square[8 * m : 8 * m + 8]
            inv[8 * g : 8 * g + 8, lines] = total

    def mixed(t):
        hi, low = hi_lo(inv[...])
        both = nn(jnp.concatenate([hi, low], axis=0).astype(BF16), mixc[t])
        return (both[64:, :128] + both[:64, 128:]) + both[:64, :128]

    def unmixed(t, cotangent):
        left = cotangent.astype(BF16)
        dinv[...] = nt(jnp.concatenate([left, left], axis=1), mixc[t])

    def message_grads(t, g, part):
        begin, rows, parts, first = PARTS[part]
        base = dinv[8 * g : 8 * g + 8, 128 * part : 128 * part + 128]
        if part == 0:
            return base
        base = base + base
        return jnp.concatenate(
            [msg[t, g, 8 * (first + m) : 8 * (first + m) + 8, :] * base for m in range(parts)],
            axis=0,
        )

    def cotangents(t, g):
        for part, (begin, rows, parts, first) in enumerate(PARTS):
            got = message_grads(t, g, part)
            dmsg[g, begin : begin + rows + 8, :] = jnp.concatenate(
                [got, jnp.zeros((8, 128), F32)], axis=0
            ).astype(BF16)

    def feature_grads(t, g):
        total = None
        for part, (begin, rows, parts, first) in enumerate(PARTS):
            lines = slice(begin, begin + rows + 8)
            dp = tn(dmsg[g, lines, :], amat[g, lines, :])
            term = dp * rad[t, 128 * part : 128 * part + 128, at(g)]
            total = term if total is None else total + term
        dcat[:, at(g)] = total.astype(BF16)

    def scattered():
        return nt(oh[...], dcat[...])

    def separation_grads(t, g):
        plain, change = [], None
        for part, (begin, rows, parts, first) in enumerate(PARTS):
            lines = slice(128 * part, 128 * part + 128)
            left = dmsg[g, begin : begin + rows + 8, :]
            if part:
                both = nn(left, pbf[t, g, lines, :])
                plain += [both[8 * m : 8 * m + 8] for m in range(parts)]
            both = nn(left, pdf[t, g, lines, :])
            for m in range(parts):
                term = both[8 * m : 8 * m + 8]
                if part:
                    term = term * row(first + m - 1, g)
                change = term if change is None else change + term
        d = plain
        ax, ay, az = row(0, g), row(1, g), row(2, g)
        change = 72.0 * change
        fx = d[0] + ROOT3 * (ay * d[3] + az * d[6] + ax * d[7]) + ax * (change - d[5])
        fy = d[1] + ROOT3 * (ax * d[3] + az * d[4] - ay * d[7]) + ay * (change - d[5])
        fz = d[2] + ROOT3 * (ay * d[4] + ax * d[6]) + az * (change + 2.0 * d[5])
        whole = jnp.concatenate([fx * diag, fy * diag, fz * diag], axis=0)
        if t == 1:
            frc[:, at(g)] = whole
        else:
            frc[:, at(g)] += whole

    arrive(send_one)
    gather_table(tab1)
    messages(0)
    z_one = mixed(0)

    def own_rows(table, cx, cy):
        return table[1 + cx, 1 + cy].astype(F32)

    for cx in range(2):
        for cy in range(2):
            first = 16 * (2 * cx + cy)
            rows = z_one[first : first + 16] + own_rows(tab1, cx, cy)
            tab2[1 + cx, 1 + cy] = rows.astype(BF16)
    start(send_two)
    radial(1)
    sent(send_pos)
    sent(send_one)
    groups(slope_rows)
    radial_grad(0)

    arrive(send_two)
    gather_table(tab2)
    messages(1)
    z_two = mixed(1) + jnp.concatenate(
        [own_rows(tab2, cx, cy) for cx in range(2) for cy in range(2)], axis=0
    )
    sig = 0.5 * jnp.tanh(0.5 * z_two) + 0.5
    silu = z_two * sig
    out = jnp.broadcast_to(readout[...], (8, 128))
    z_grad = (sig + silu * (1.0 - sig)) * readout[...]
    unmixed(1, z_grad)
    groups(cotangents, 1)
    groups(feature_grads, 1)

    def put_ghosts(target, full):
        for hx in range(4):
            for hy in range(4):
                if hx in (1, 2) and hy in (1, 2):
                    continue
                first = 16 * (4 * hx + hy)
                target[hx, hy] = full[first : first + 16].astype(target.dtype)

    full = scattered()
    put_ghosts(gs2, full)
    start(back_two)

    values = lax.dot_general(
        out, silu, (((1,), (1,)), ((), ())),
        precision=lax.Precision.HIGHEST, preferred_element_type=F32,
    )
    for cx in range(2):
        for cy in range(2):
            first = 16 * (2 * cx + cy)
            energy[cx, cy : cy + 1, :] = values[0:1, first : first + 16]

    def own_block(full):
        return jnp.concatenate(
            [full[16 * (4 * hx + hy) : 16 * (4 * hx + hy) + 16] for hx in (1, 2) for hy in (1, 2)],
            axis=0,
        )

    own_two = z_grad + own_block(full)
    radial_grad(1)
    groups(separation_grads, 1)

    def returned(target, cx, cy):
        hx, hy = 3 * cx, 3 * cy
        return (
            target[hx, 1 + cy].astype(F32)
            + target[1 + cx, hy].astype(F32)
            + target[hx, hy].astype(F32)
        )

    sent(send_two)
    arrive(back_two)
    own_two = own_two + jnp.concatenate(
        [returned(gr2, cx, cy) for cx in range(2) for cy in range(2)], axis=0
    )
    unmixed(0, own_two)
    groups(cotangents, 0)
    groups(feature_grads, 0)
    full = scattered()
    put_ghosts(gs1, full)
    start(back_one)
    own_one = own_two + own_block(full)
    groups(separation_grads, 0)

    hi, low = hi_lo(frc[...])
    both = nt(jnp.concatenate([hi, low], axis=0).astype(BF16), signed[...])
    both = both[:24] + both[24:]
    moved = jnp.concatenate(
        [jnp.sum(both[8 * c : 8 * c + 8], axis=0, keepdims=True) for c in range(3)], axis=0
    ) * (1.0 / 6.0)
    for hx in range(4):
        for hy in range(4):
            if hx in (1, 2) and hy in (1, 2):
                continue
            first = 16 * (4 * hx + hy)
            ps[hx, hy] = moved[:, first : first + 16]
    start(back_pos)

    sent(back_two)
    arrive(back_one)
    for cx in range(2):
        for cy in range(2):
            first = 16 * (2 * cx + cy)
            fgrad[cx, cy] = own_one[first : first + 16] + returned(gr1, cx, cy)

    arrive(back_pos)
    for cx in range(2):
        for cy in range(2):
            first = 16 * (4 * (1 + cx) + 1 + cy)
            total = -(moved[:, first : first + 16] + returned(pr, cx, cy))
            for comp in range(3):
                forces[cx, comp, cy : cy + 1, :] = total[comp : comp + 1]

    sent(back_one)
    sent(back_pos)


def deliver(a, b, c, a_out, b_out, c_out, sem):
    moves = [
        pltpu.make_async_copy(source, target, sem.at[k])
        for k, (source, target) in enumerate(((a, a_out), (b, b_out), (c, c_out)))
    ]
    for move in moves:
        move.start()
    for move in moves:
        move.wait()


def scratch():
    vmem = pltpu.VMEM
    return [
        vmem((2, 2, 16, 128), BF16),
        vmem((2, 3, 2, 16), F32),
        vmem((2, 2, 16), jnp.int32),
        vmem((2, 2, 16, 32), jnp.int32),
        vmem((2, 2, 16), jnp.int32),
        vmem((6, 128), F32),
        vmem((2, 8, 64), F32),
        vmem((2, 64, 384), F32),
        vmem((2, 384, 128), F32),
        vmem((1, 128), F32),
        vmem((4, 4, 16, 128), BF16),
        vmem((4, 4, 16, 128), BF16),
        vmem((4, 4, 3, 128), F32),
        vmem((4, 4, 3, 128), F32),
        vmem((4, 4, 16, 128), GRAD),
        vmem((4, 4, 16, 128), GRAD),
        vmem((4, 4, 16, 128), GRAD),
        vmem((4, 4, 16, 128), GRAD),
        vmem((4, 4, 3, 16), F32),
        vmem((4, 4, 3, 16), F32),
        vmem((256, 2048), BF16),
        vmem((256, 2048), BF16),
        vmem((8, 96, 256), BF16),
        vmem((12, 8, 256), F32),
        vmem((8, 16), F32),
        vmem((2, 8, 64, 256), F32),
        vmem((2, 8, 64, 256), F32),
        vmem((2, 384, 2048), F32),
        vmem((2, 8, 384, 256), BF16),
        vmem((2, 8, 384, 256), BF16),
        vmem((2, 128, 2048), F32),
        vmem((2, 8, 72, 128), F32),
        vmem((64, 384), F32),
        vmem((64, 384), F32),
        vmem((128, 2048), BF16),
        vmem((24, 2048), F32),
        vmem((2, 384, 128), BF16),
        vmem((2, 32, 64), BF16),
        vmem((2, 384, 256), BF16),
        vmem((128, 256), BF16),
        vmem((128, 2048), BF16),
        vmem((32, 2048), BF16),
        vmem((64, 2048), F32),
        vmem((8, 96, 128), BF16),
        pltpu.SemaphoreType.DMA((10,)),
        pltpu.SemaphoreType.DMA((6, 8)),
        pltpu.SemaphoreType.DMA((6, 8)),
    ]


def shards(nx, ny, features, positions, species, neighbours, counts, gain, w_in, w_out, mix, readout):
    shape = jax.ShapeDtypeStruct
    outside = pl.BlockSpec(memory_space=pl.ANY)
    whole = pl.BlockSpec(memory_space=pltpu.VMEM)
    energy, forces, fgrad = pl.pallas_call(
        functools.partial(kernel, nx, ny),
        out_shape=(
            pltpu.VMEM((2, 2, 16), F32),
            pltpu.VMEM((2, 3, 2, 16), F32),
            pltpu.VMEM((2, 2, 16, 128), F32),
        ),
        in_specs=[outside] * 10,
        out_specs=(whole,) * 3,
        scratch_shapes=scratch(),
        compiler_params=pltpu.CompilerParams(
            collective_id=0, has_side_effects=True, vmem_limit_bytes=VLIM * 1024 * 1024
        ),
        name="potential",
    )(
        features, jnp.transpose(positions, (0, 2, 1, 3)), species, neighbours, counts, gain,
        w_in, w_out, mix, readout.reshape(1, -1),
    )
    results = (energy, forces, fgrad)
    energy, forces, fgrad = pl.pallas_call(
        deliver,
        out_shape=tuple(shape(x.shape, x.dtype) for x in results),
        in_specs=[whole] * 3,
        out_specs=(pl.BlockSpec(memory_space=pltpu.HBM),) * 3,
        scratch_shapes=[pltpu.SemaphoreType.DMA((3,))],
        compiler_params=pltpu.CompilerParams(vmem_limit_bytes=1024 * 1024),
        name="deliver",
    )(*results)
    return energy, jnp.transpose(forces, (0, 2, 1, 3)), fgrad


def solution(mesh):
    placed = (
        P("gx", "gy", None, None), P("gx", "gy", None, None), P("gx", "gy", None),
        P("gx", "gy", None, None), P("gx", "gy", None), P(), P(), P(), P(), P(),
    )
    return jax.shard_map(
        functools.partial(shards, mesh.shape["gx"], mesh.shape["gy"]),
        mesh=mesh,
        in_specs=placed,
        out_specs=(P("gx", "gy", None), P("gx", "gy", None, None), P("gx", "gy", None, None)),
        check_vma=False,
    )
```

```python
import functools

import jax
import jax.numpy as jnp
from jax import lax
from jax.experimental import pallas as pl
from jax.experimental.pallas import tpu as pltpu
from jax.sharding import PartitionSpec as P

F32 = jnp.float32
BF16 = jnp.bfloat16
MESH = pl.DeviceIdType.MESH
GRAD = BF16
DIRS = ((1, 1), (1, -1), (-1, 1), (-1, -1), (1, 0), (-1, 0), (0, 1), (0, -1))
VLIM = 60
SPACING = 6.0 / 7.0
ROOT3 = 3.0**0.5
GROUPS = 8
PARTS = ((0, 8, 1, 0), (16, 24, 3, 1), (48, 40, 5, 4))


def nn(a, b):
    return lax.dot_general(a, b, (((1,), (0,)), ((), ())), preferred_element_type=F32)


def nt(a, b):
    return lax.dot_general(a, b, (((1,), (1,)), ((), ())), preferred_element_type=F32)


def tn(a, b):
    return lax.dot_general(a, b, (((0,), (0,)), ((), ())), preferred_element_type=F32)


def hi_lo(x):
    hi = x.astype(BF16).astype(F32)
    return hi, x - hi


def three(x):
    hi, rest = hi_lo(x)
    mid, low = hi_lo(rest)
    return hi, mid, low


def iota(shape, dim):
    return lax.broadcasted_iota(jnp.int32, shape, dim)


def kernel(
    nx, ny,
    feat_h, pos_h, spec_h, nb_h, cnt_h, gain_h, w_in_h, w_out_h, mix_h, readout_h,
    energy, forces, fgrad,
    feat, pos, spec, nb, cnt, gain, w_in, w_out, mix, readout,
    tab1, tab2, postab, gs2, gr2, gs1, gr1, ps, pr,
    oh, signed, amat, geo, atom, hid, dse, rad, pbf, pdf, xjt, msg, inv, dinv, dcat, frc,
    wo3, w3, mixc, tabt, units, basis, pre, dmsg,
    lsem, ssem, rsem,
):
    gx, gy = lax.axis_index("gx"), lax.axis_index("gy")
    rows = {0: gx, 1: lax.rem(gx + 1, nx), -1: lax.rem(gx + (nx - 1), nx)}
    cols = {0: gy, 1: lax.rem(gy + 1, ny), -1: lax.rem(gy + (ny - 1), ny)}
    peers = [(rows[dx], cols[dy]) for dx, dy in DIRS]

    barrier = pltpu.get_barrier_semaphore()
    for peer in peers:
        pl.semaphore_signal(barrier, inc=1, device_id=peer, device_id_type=MESH)

    def pick(d, up, down, mid):
        return up if d == 1 else down if d == -1 else mid

    def copies(slot, src, dst, src_at, dst_at):
        out = []
        for k, (dx, dy) in enumerate(DIRS):
            out.append(
                pltpu.make_async_remote_copy(
                    src_ref=src.at[src_at(dx), src_at(dy)],
                    dst_ref=dst.at[dst_at(dx), dst_at(dy)],
                    send_sem=ssem.at[slot, k],
                    recv_sem=rsem.at[slot, k],
                    device_id=peers[k],
                    device_id_type=MESH,
                )
            )
        return out

    centre = pl.ds(1, 2)

    def owned_at(d):
        return pick(d, 2, 1, centre)

    def halo_at(d):
        return pick(d, 0, 3, centre)

    def ghost_at(d):
        return pick(d, 3, 0, centre)

    send_pos = copies(0, postab, postab, owned_at, halo_at)
    send_one = copies(1, tab1, tab1, owned_at, halo_at)
    send_two = copies(2, tab2, tab2, owned_at, halo_at)
    back_two = copies(3, gs2, gr2, ghost_at, halo_at)
    back_one = copies(4, gs1, gr1, ghost_at, halo_at)
    back_pos = copies(5, ps, pr, ghost_at, halo_at)

    def start(group):
        for copy in group:
            copy.start()

    def arrive(group):
        for copy in group:
            copy.wait_recv()

    sources = (pos_h, spec_h, feat_h, gain_h, nb_h, cnt_h, w_in_h, w_out_h, mix_h, readout_h)
    targets = (pos, spec, feat, gain, nb, cnt, w_in, w_out, mix, readout)
    loads = [
        pltpu.make_async_copy(source, target, lsem.at[k])
        for k, (source, target) in enumerate(zip(sources, targets))
    ]
    start(loads)

    loads[0].wait()
    for cx in range(2):
        for cy in range(2):
            for comp in range(3):
                postab[1 + cx, 1 + cy, comp : comp + 1, :] = pos[cx, comp, cy : cy + 1, :]
    for k in (1, 2, 3):
        loads[k].wait()
    kinds = gain.shape[0]
    for cx in range(2):
        for cy in range(2):
            onehot = (iota((kinds, 16), 0) == spec[cx, cy : cy + 1, :]).astype(F32)
            rows = lax.dot_general(
                onehot, gain[...], (((0,), (0,)), ((), ())),
                precision=lax.Precision.HIGHEST, preferred_element_type=F32,
            )
            tab1[1 + cx, 1 + cy] = (feat[cx, cy].astype(F32) * rows).astype(BF16)

    pl.semaphore_wait(barrier, len(DIRS))
    start(send_pos)
    start(send_one)

    for k in (4, 5):
        loads[k].wait()
    sub = iota((8, 256), 0)
    lane = iota((8, 256), 1)
    lane_atom = lax.shift_right_logical(lane, 5)
    diag = (sub == lane_atom).astype(F32)
    codes = nb[...].reshape(64, 32).astype(F32).astype(BF16)
    tile = (iota((32, 256), 0) == (iota((32, 256), 1) & 31)).astype(BF16)
    repeated = nn(codes, tile)
    keep = (iota((64, 256), 0) & 7) == lax.shift_right_logical(iota((64, 256), 1), 5)
    repeated = jnp.where(keep, repeated, 0.0).astype(BF16)
    gather8 = (iota((8, 64), 0) == lax.shift_right_logical(iota((8, 64), 1), 3)).astype(BF16)
    code = nn(gather8, repeated).astype(jnp.int32)
    offset = lax.shift_right_logical(code, 4)
    step_x = (offset >= 3).astype(jnp.int32) + (offset >= 6).astype(jnp.int32)
    step_y = offset - 3 * step_x
    halo_x = lax.shift_right_logical(sub, 2) + step_x
    halo_y = (lax.shift_right_logical(sub, 1) & 1) + step_y
    index = (halo_x * 4 + halo_y) * 16 + (code & 15)

    for g in range(GROUPS):
        atom[g : g + 1, :] = cnt[g // 4, g // 2 % 2 : g // 2 % 2 + 1, :].astype(F32)
    half16 = lax.shift_right_logical(iota((8, 16), 1), 3) == (iota((8, 16), 0) & 1)
    spread = (
        (iota((16, 256), 0) & 7) == lax.shift_right_logical(iota((16, 256), 1), 5)
    ).astype(BF16)
    count = nn(jnp.where(half16, atom[...], 0.0).astype(BF16), spread)
    live = ((lane & 31).astype(F32) < count).astype(F32)

    def at(g):
        return slice(256 * g, 256 * g + 256)

    candidate = iota((256, 256), 0)
    for g in range(GROUPS):
        found = (candidate == index[g : g + 1]).astype(F32)
        oh[:, at(g)] = found.astype(BF16)
        mine = 16 * (4 * (1 + g // 4) + 1 + g // 2 % 2) + 8 * (g % 2)
        signed[:, at(g)] = jnp.concatenate(
            [found[:mine], found[mine : mine + 8] - diag, found[mine + 8 :]], axis=0
        ).astype(BF16)

    for k in (6, 7, 8, 9):
        loads[k].wait()
    for t in range(2):
        hi, low = hi_lo(w_out[t])
        wo3[t] = jnp.concatenate([hi, low], axis=0).T.astype(BF16)
        hi, low = hi_lo(w_in[t])
        w3[t] = jnp.concatenate([hi, hi, low, low], axis=0).astype(BF16)
        hi, low = hi_lo(mix[t])
        mixc[t] = jnp.concatenate([hi, low], axis=1).astype(BF16)

    arrive(send_pos)
    spots = [postab[hx, hy] for hx in range(4) for hy in range(4)]
    lanes = jnp.concatenate(spots, axis=1)
    lanes = jnp.concatenate([lanes, jnp.zeros((5, 256), F32)], axis=0)
    split = jnp.concatenate(list(three(lanes)) + [jnp.zeros((8, 256), F32)], axis=0).astype(BF16)
    for g in range(GROUPS):
        found = nn(split, signed[:, at(g)])
        found = found[0:8] + (found[8:16] + found[16:24])
        for comp in range(3):
            geo[comp, g : g + 1, :] = found[comp : comp + 1]
    ux = geo[0] / 6.0 + (step_x - 1).astype(F32)
    uy = geo[1] / 6.0 + (step_y - 1).astype(F32)
    uz = geo[2] / 6.0
    unit_sq = ux * ux + uy * uy + uz * uz
    distance = jnp.sqrt(36.0 * unit_sq + 0.01)
    inside = jnp.maximum(1.0 - unit_sq, 0.0)
    inside_live = inside * live
    geo[0] = ux
    geo[1] = uy
    geo[2] = uz
    geo[3] = ROOT3 * ux * uy
    geo[4] = ROOT3 * uy * uz
    geo[5] = uz * uz - 0.5 * (ux * ux + uy * uy)
    geo[6] = ROOT3 * ux * uz
    geo[7] = 0.5 * ROOT3 * (ux * ux - uy * uy)
    geo[8] = distance / SPACING
    geo[9] = inside * inside_live
    geo[10] = -1.0 / (SPACING * distance)
    geo[11] = (-2.0 / 36.0) * inside_live

    def row(q, g):
        return geo[q, g : g + 1, :]

    order = iota((8, 256), 0).astype(F32)

    def four_basis(x):
        hi, low = hi_lo(x)
        return jnp.concatenate([hi, low, hi, low], axis=0).astype(BF16)

    def basis_rows(g):
        arg = row(8, g) - order
        basis[:, at(g)] = four_basis(jnp.exp(-(arg * arg)))

    def slope_rows(g):
        arg = row(8, g) - order
        basis[:, at(g)] = four_basis(jnp.exp(-(arg * arg)) * arg * row(10, g))

    def radial(t):
        pre[...] = tn(w3[t], basis[...])
        groups(hidden_units, t)
        rad[t] = nn(wo3[t], units[...])

    def hidden_units(t, g):
        envelope = row(9, g)
        value = pre[:, at(g)]
        sig = 0.5 * jnp.tanh(0.5 * value) + 0.5
        silu = value * sig
        hid[t, g] = silu
        dse[t, g] = sig
        half = (silu * envelope).astype(BF16)
        units[:, at(g)] = jnp.concatenate([half, half], axis=0)

    def radial_grad(t):
        pre[...] = tn(w3[t], basis[...])
        groups(unit_slopes, t)
        groups(radial_change, t)

    def unit_slopes(t, g):
        dpre = pre[:, at(g)]
        sig, silu = dse[t, g], hid[t, g]
        slope = (sig + silu * (1.0 - sig)) * row(9, g)
        half = (slope * dpre + silu * row(11, g)).astype(BF16)
        units[:, at(g)] = jnp.concatenate([half, half], axis=0)

    def radial_change(t, g):
        change = nn(wo3[t], units[:, at(g)])
        found = xjt[t, :, at(g)]
        for part in range(3):
            lines = slice(128 * part, 128 * part + 128)
            pdf[t, g, lines, :] = (change[lines] * found).astype(BF16)

    def make_harmonics(g):
        rows = []
        for _, _, parts, first in PARTS:
            rows += [row(first + m - 1, g) * diag if first else diag for m in range(parts)]
            rows += [jnp.zeros_like(diag)]
        amat[g] = jnp.concatenate(rows, axis=0).astype(BF16)

    def groups(body, *args):
        for g in range(GROUPS):
            body(*args, g)

    groups(basis_rows)
    radial(0)
    groups(make_harmonics)

    def gather_table(table):
        tabt[...] = table[...].reshape(256, 128).astype(F32).T.astype(BF16)

    def messages(t):
        xjt[t] = nn(tabt[...], oh[...])
        groups(products, t)
        groups(message_sums, t)

    def products(t, g):
        found = xjt[t, :, at(g)]
        for part in range(3):
            lines = slice(128 * part, 128 * part + 128)
            pbf[t, g, lines, :] = (rad[t, lines, at(g)] * found).astype(BF16)

    def message_sums(t, g):
        for part, (begin, rows, parts, first) in enumerate(PARTS):
            lines = slice(128 * part, 128 * part + 128)
            got = nt(amat[g, begin : begin + rows + 8, :], pbf[t, g, lines, :])[:rows]
            msg[t, g, 8 * first : 8 * first + rows, :] = got
            if part == 0:
                total = got
            else:
                square = got * got
                total = square[0:8]
                for m in range(1, parts):
                    total = total + square[8 * m : 8 * m + 8]
            inv[8 * g : 8 * g + 8, lines] = total

    def mixed(t):
        hi, low = hi_lo(inv[...])
        both = nn(jnp.concatenate([hi, low], axis=0).astype(BF16), mixc[t])
        return (both[64:, :128] + both[:64, 128:]) + both[:64, :128]

    def unmixed(t, cotangent):
        left = cotangent.astype(BF16)
        dinv[...] = nt(jnp.concatenate([left, left], axis=1), mixc[t])

    def message_grads(t, g, part):
        begin, rows, parts, first = PARTS[part]
        base = dinv[8 * g : 8 * g + 8, 128 * part : 128 * part + 128]
        if part == 0:
            return base
        base = base + base
        return jnp.concatenate(
            [msg[t, g, 8 * (first + m) : 8 * (first + m) + 8, :] * base for m in range(parts)],
            axis=0,
        )

    def cotangents(t, g):
        for part, (begin, rows, parts, first) in enumerate(PARTS):
            got = message_grads(t, g, part)
            dmsg[g, begin : begin + rows + 8, :] = jnp.concatenate(
                [got, jnp.zeros((8, 128), F32)], axis=0
            ).astype(BF16)

    def feature_grads(t, g):
        total = None
        for part, (begin, rows, parts, first) in enumerate(PARTS):
            lines = slice(begin, begin + rows + 8)
            dp = tn(dmsg[g, lines, :], amat[g, lines, :])
            term = dp * rad[t, 128 * part : 128 * part + 128, at(g)]
            total = term if total is None else total + term
        dcat[:, at(g)] = total.astype(BF16)

    def scattered():
        return nt(oh[...], dcat[...])

    def separation_grads(t, g):
        plain, change = [], None
        for part, (begin, rows, parts, first) in enumerate(PARTS):
            lines = slice(128 * part, 128 * part + 128)
            left = dmsg[g, begin : begin + rows + 8, :]
            if part:
                both = nn(left, pbf[t, g, lines, :])
                plain += [both[8 * m : 8 * m + 8] for m in range(parts)]
            both = nn(left, pdf[t, g, lines, :])
            for m in range(parts):
                term = both[8 * m : 8 * m + 8]
                if part:
                    term = term * row(first + m - 1, g)
                change = term if change is None else change + term
        d = plain
        ax, ay, az = row(0, g), row(1, g), row(2, g)
        change = 72.0 * change
        fx = d[0] + ROOT3 * (ay * d[3] + az * d[6] + ax * d[7]) + ax * (change - d[5])
        fy = d[1] + ROOT3 * (ax * d[3] + az * d[4] - ay * d[7]) + ay * (change - d[5])
        fz = d[2] + ROOT3 * (ay * d[4] + ax * d[6]) + az * (change + 2.0 * d[5])
        whole = jnp.concatenate([fx * diag, fy * diag, fz * diag], axis=0)
        if t == 1:
            frc[:, at(g)] = whole
        else:
            frc[:, at(g)] += whole

    arrive(send_one)
    gather_table(tab1)
    messages(0)
    z_one = mixed(0)

    def own_rows(table, cx, cy):
        return table[1 + cx, 1 + cy].astype(F32)

    for cx in range(2):
        for cy in range(2):
            first = 16 * (2 * cx + cy)
            rows = z_one[first : first + 16] + own_rows(tab1, cx, cy)
            tab2[1 + cx, 1 + cy] = rows.astype(BF16)
    start(send_two)
    radial(1)
    groups(slope_rows)
    radial_grad(0)

    arrive(send_two)
    gather_table(tab2)
    messages(1)
    z_two = mixed(1) + jnp.concatenate(
        [own_rows(tab2, cx, cy) for cx in range(2) for cy in range(2)], axis=0
    )
    sig = 0.5 * jnp.tanh(0.5 * z_two) + 0.5
    silu = z_two * sig
    out = jnp.broadcast_to(readout[...], (8, 128))
    z_grad = (sig + silu * (1.0 - sig)) * readout[...]
    unmixed(1, z_grad)
    groups(cotangents, 1)
    groups(feature_grads, 1)

    def put_ghosts(target, full):
        for hx in range(4):
            for hy in range(4):
                if hx in (1, 2) and hy in (1, 2):
                    continue
                first = 16 * (4 * hx + hy)
                target[hx, hy] = full[first : first + 16].astype(target.dtype)

    full = scattered()
    put_ghosts(gs2, full)
    start(back_two)

    values = lax.dot_general(
        out, silu, (((1,), (1,)), ((), ())),
        precision=lax.Precision.HIGHEST, preferred_element_type=F32,
    )
    for cx in range(2):
        for cy in range(2):
            first = 16 * (2 * cx + cy)
            energy[cx, cy : cy + 1, :] = values[0:1, first : first + 16]

    def own_block(full):
        return jnp.concatenate(
            [full[16 * (4 * hx + hy) : 16 * (4 * hx + hy) + 16] for hx in (1, 2) for hy in (1, 2)],
            axis=0,
        )

    own_two = z_grad + own_block(full)
    radial_grad(1)
    groups(separation_grads, 1)

    def returned(target, cx, cy):
        hx, hy = 3 * cx, 3 * cy
        return (
            target[hx, 1 + cy].astype(F32)
            + target[1 + cx, hy].astype(F32)
            + target[hx, hy].astype(F32)
        )

    arrive(back_two)
    own_two = own_two + jnp.concatenate(
        [returned(gr2, cx, cy) for cx in range(2) for cy in range(2)], axis=0
    )
    unmixed(0, own_two)
    groups(cotangents, 0)
    groups(separation_grads, 0)

    hi, low = hi_lo(frc[...])
    both = nt(jnp.concatenate([hi, low], axis=0).astype(BF16), signed[...])
    both = both[:24] + both[24:]
    moved = jnp.concatenate(
        [jnp.sum(both[8 * c : 8 * c + 8], axis=0, keepdims=True) for c in range(3)], axis=0
    ) * (1.0 / 6.0)
    for hx in range(4):
        for hy in range(4):
            if hx in (1, 2) and hy in (1, 2):
                continue
            first = 16 * (4 * hx + hy)
            ps[hx, hy] = moved[:, first : first + 16]
    start(back_pos)
    groups(feature_grads, 0)
    full = scattered()
    put_ghosts(gs1, full)
    start(back_one)
    own_one = own_two + own_block(full)

    arrive(back_pos)
    for cx in range(2):
        for cy in range(2):
            first = 16 * (4 * (1 + cx) + 1 + cy)
            total = -(moved[:, first : first + 16] + returned(pr, cx, cy))
            for comp in range(3):
                forces[cx, comp, cy : cy + 1, :] = total[comp : comp + 1]

    arrive(back_one)
    for cx in range(2):
        for cy in range(2):
            first = 16 * (2 * cx + cy)
            fgrad[cx, cy] = own_one[first : first + 16] + returned(gr1, cx, cy)

    for group in (send_pos, send_one, send_two, back_two, back_one, back_pos):
        for copy in group:
            copy.wait_send()


def deliver(a, b, c, a_out, b_out, c_out, sem):
    moves = [
        pltpu.make_async_copy(source, target, sem.at[k])
        for k, (source, target) in enumerate(((a, a_out), (b, b_out), (c, c_out)))
    ]
    for move in moves:
        move.start()
    for move in moves:
        move.wait()


def scratch():
    vmem = pltpu.VMEM
    return [
        vmem((2, 2, 16, 128), BF16),
        vmem((2, 3, 2, 16), F32),
        vmem((2, 2, 16), jnp.int32),
        vmem((2, 2, 16, 32), jnp.int32),
        vmem((2, 2, 16), jnp.int32),
        vmem((6, 128), F32),
        vmem((2, 8, 64), F32),
        vmem((2, 64, 384), F32),
        vmem((2, 384, 128), F32),
        vmem((1, 128), F32),
        vmem((4, 4, 16, 128), BF16),
        vmem((4, 4, 16, 128), BF16),
        vmem((4, 4, 3, 16), F32),
        vmem((4, 4, 16, 128), GRAD),
        vmem((4, 4, 16, 128), GRAD),
        vmem((4, 4, 16, 128), GRAD),
        vmem((4, 4, 16, 128), GRAD),
        vmem((4, 4, 3, 16), F32),
        vmem((4, 4, 3, 16), F32),
        vmem((256, 2048), BF16),
        vmem((256, 2048), BF16),
        vmem((8, 96, 256), BF16),
        vmem((12, 8, 256), F32),
        vmem((8, 16), F32),
        vmem((2, 8, 64, 256), F32),
        vmem((2, 8, 64, 256), F32),
        vmem((2, 384, 2048), F32),
        vmem((2, 8, 384, 256), BF16),
        vmem((2, 8, 384, 256), BF16),
        vmem((2, 128, 2048), F32),
        vmem((2, 8, 72, 128), F32),
        vmem((64, 384), F32),
        vmem((64, 384), F32),
        vmem((128, 2048), BF16),
        vmem((24, 2048), F32),
        vmem((2, 384, 128), BF16),
        vmem((2, 32, 64), BF16),
        vmem((2, 384, 256), BF16),
        vmem((128, 256), BF16),
        vmem((128, 2048), BF16),
        vmem((32, 2048), BF16),
        vmem((64, 2048), F32),
        vmem((8, 96, 128), BF16),
        pltpu.SemaphoreType.DMA((10,)),
        pltpu.SemaphoreType.DMA((6, 8)),
        pltpu.SemaphoreType.DMA((6, 8)),
    ]


def shards(nx, ny, features, positions, species, neighbours, counts, gain, w_in, w_out, mix, readout):
    shape = jax.ShapeDtypeStruct
    outside = pl.BlockSpec(memory_space=pl.ANY)
    whole = pl.BlockSpec(memory_space=pltpu.VMEM)
    energy, forces, fgrad = pl.pallas_call(
        functools.partial(kernel, nx, ny),
        out_shape=(
            pltpu.VMEM((2, 2, 16), F32),
            pltpu.VMEM((2, 3, 2, 16), F32),
            pltpu.VMEM((2, 2, 16, 128), F32),
        ),
        in_specs=[outside] * 10,
        out_specs=(whole,) * 3,
        scratch_shapes=scratch(),
        compiler_params=pltpu.CompilerParams(
            collective_id=0, has_side_effects=True, vmem_limit_bytes=VLIM * 1024 * 1024
        ),
        name="potential",
    )(
        features, jnp.transpose(positions, (0, 2, 1, 3)), species, neighbours, counts, gain,
        w_in, w_out, mix, readout.reshape(1, -1),
    )
    results = (energy, forces, fgrad)
    energy, forces, fgrad = pl.pallas_call(
        deliver,
        out_shape=tuple(shape(x.shape, x.dtype) for x in results),
        in_specs=[whole] * 3,
        out_specs=(pl.BlockSpec(memory_space=pltpu.HBM),) * 3,
        scratch_shapes=[pltpu.SemaphoreType.DMA((3,))],
        compiler_params=pltpu.CompilerParams(vmem_limit_bytes=1024 * 1024),
        name="deliver",
    )(*results)
    return energy, jnp.transpose(forces, (0, 2, 1, 3)), fgrad


def solution(mesh):
    placed = (
        P("gx", "gy", None, None), P("gx", "gy", None, None), P("gx", "gy", None),
        P("gx", "gy", None, None), P("gx", "gy", None), P(), P(), P(), P(), P(),
    )
    return jax.shard_map(
        functools.partial(shards, mesh.shape["gx"], mesh.shape["gy"]),
        mesh=mesh,
        in_specs=placed,
        out_specs=(P("gx", "gy", None), P("gx", "gy", None, None), P("gx", "gy", None, None)),
        check_vma=False,
    )
```
